512 devices in a mesh: slide: 128 (over x, z, core), rep: 4 (over y).
Axes of the slice: x: 4, y: 4, z: 16, core: 2. Of those that a mesh axis runs over, the one named last changes fastest.
Arguments:
- tile_feats: bfloat16 [2048, 8, 8, 192], P(('slide', 'rep'))
- cotangent: bfloat16 [2048, 4, 4, 384], P(('slide', 'rep')), may hold values from -0.03125 to 0.03125
- keep_list: int32 [512, 4], P(('slide', 'rep')), may hold values from 0 to 3, each once within a row
- tile_plan: int32 [512, 2], P(('slide', 'rep')), may hold values from 0 to 4, as said below
- kernel_one: bfloat16 [7, 7, 192], replicated, may hold values from -0.875 to 0.875
- gain_one: bfloat16 [192], replicated, may hold values from 0.25 to 1.75
- inward_one: bfloat16 [192, 768], replicated, may hold values from -0.4375 to 0.4375
- outward_one: bfloat16 [768, 192], replicated, may hold values from -0.21875 to 0.21875
- gain_down: bfloat16 [192], replicated, may hold values from 0.25 to 1.75
- project_down: bfloat16 [768, 384], replicated, may hold values from -0.21875 to 0.21875
- kernel_two: bfloat16 [7, 7, 384], replicated, may hold values from -0.875 to 0.875
- gain_two: bfloat16 [384], replicated, may hold values from 0.25 to 1.75
- inward_two: bfloat16 [384, 1536], replicated, may hold values from -0.3125 to 0.3125
- outward_two: bfloat16 [1536, 384], replicated, may hold values from -0.15625 to 0.15625
Outputs:
- features: bfloat16 [2048, 4, 4, 384], P(('slide', 'rep'))
- grad_inward: float32 [192, 768], P(None, 'slide')
- grad_outward: float32 [768, 192], P('slide')
- grad_project: float32 [768, 384], P('slide')
The draws below stay inside these ranges and needn't reach their ends.
Inputs may be any that keep to these rules, and one draw needn't show every extreme that they name: `keep_list`: each row is a permutation of 0 to 3. `tile_plan`: column 0 counts the device's kept tiles, column 1 is its partner bit, from 0 to 2. The device at the same rep index whose slide index differs only in that bit is its partner and has the same partner bit; the bit is the same over each aligned group of 8 slide indices. Partners' counts sum to at most 4. In every replica some device keeps 4 tiles and its partner none.
All inputs are finite; a program needn't handle non-finite values.
Results may differ from the reference program's by a relative error of at most 0.018.
Values may be sent and summed in bfloat16 or wider, within the bound.
No kernel may reach another device: no remote copies, remote signals or barrier semaphores. Data moves between devices by JAX's collectives and lax.ppermute only.
A program may use at most 64 MiB of HBM per device.

```python
import jax
import jax.numpy as jnp
from jax import lax

C1 = 192
C2 = 384
KSIZE = 7
HID1 = 768
HID2 = 1536
S1 = 8
S2 = 4
CAP = 2
CAND = 4
SLIDES = 128
REPLICAS = 4
GROUPS = 512
TILES = 2048


def draw_tile_feats(key, part):
    first, second, third = jax.random.split(key, 3)
    shape = (TILES, S1, S1, C1)
    base = jax.random.normal(first, shape, jnp.float32)
    channel = jnp.exp(jax.random.uniform(second, (C1,), jnp.float32, 0.0, 2.3)) * 0.3
    cell = jnp.exp(jax.random.uniform(third, (TILES, S1, S1, 1), jnp.float32, 0.0, 2.3)) * 0.3
    return (base * channel * cell).astype(jnp.bfloat16)


def draw_tile_plan(key, part):
    base = jax.random.fold_in(key, 11)
    first, second, third, fourth = jax.random.split(base, 4)
    slide_index = jnp.arange(SLIDES, dtype=jnp.int32)[:, None] + jnp.zeros((1, REPLICAS), jnp.int32)
    replica = jnp.arange(REPLICAS, dtype=jnp.int32)[None, :] + jnp.zeros((SLIDES, 1), jnp.int32)
    bit_table = jax.random.randint(first, (SLIDES // 8, REPLICAS), 0, 3)
    bit_table = bit_table.at[0, 0].set(2).at[0, 1].set(0)
    partner_bits = bit_table[slide_index // 8, replica]
    stride = jnp.left_shift(jnp.ones_like(partner_bits), partner_bits)
    upper = slide_index // stride % 2
    leader = slide_index - upper * stride
    kinds = jax.random.randint(second, (SLIDES, REPLICAS), 0, 3)[leader, replica]
    kinds = jnp.where(leader == 0, 0, kinds)
    flips = jax.random.randint(third, (SLIDES, REPLICAS), 0, 2)[leader, replica]
    spares = jax.random.randint(fourth, (SLIDES, REPLICAS), 0, CAP + 1)[leader, replica]
    heavy = jnp.where(kinds == 0, 2 * CAP, jnp.where(kinds == 1, 2 * CAP - 1, CAP))
    light = jnp.where(kinds == 0, 0, jnp.where(kinds == 1, 1, spares))
    counts = jnp.where(upper == flips, heavy, light)
    return jnp.stack([counts, partner_bits], axis=-1).reshape(SLIDES * REPLICAS, 2).astype(jnp.int32)


def levels(rng, dims, pieces, low, top_value):
    level = 1.0
    for dim, parts in pieces:
        heights = jax.random.uniform(jax.random.fold_in(jax.random.fold_in(rng, 6), dim), (parts,), jnp.float32, low / len(pieces), top_value / len(pieces))
        level = level * jnp.repeat(jnp.exp(heights), dims[dim] // parts).reshape((-1,) + (1,) * (len(dims) - 1 - dim))
    return level


def centred(key, extent, width, reach, cuts=(), kind=jnp.bfloat16):
    drawn = width * jax.random.normal(key, extent, jnp.float32)
    if cuts:
        drawn = drawn * levels(key, extent, cuts, -0.22, 0.18)
    return jnp.clip(drawn, -reach, reach).astype(kind)


def setup_inputs(seed: int = 0) -> dict:
    seeds = jax.random.split(jax.random.key(seed), 15)
    return {
        "tile_feats": draw_tile_feats(jax.random.fold_in(seeds[14], 71), 0),
        "cotangent": centred(seeds[1], (TILES, S2, S2, C2), (2.0 * (S1 * S1 * CAND * GROUPS) ** -0.5), 0.03125, ((0, 512),)),
        "keep_list": jax.vmap(lambda own: jax.random.permutation(own, CAND))(jax.random.split(seeds[2], GROUPS)).reshape((GROUPS, CAND)).astype(jnp.int32),
        "tile_plan": draw_tile_plan(jax.random.fold_in(seeds[14], 71), 0),
        "kernel_one": centred(seeds[4], (KSIZE, KSIZE, C1), (KSIZE * KSIZE) ** -0.5, 0.875),
        "gain_one": jnp.clip(1.0 + 0.15 * jax.random.normal(seeds[5], (C1,), jnp.float32), 0.25, 1.75).astype(jnp.bfloat16),
        "inward_one": centred(seeds[6], (C1, HID1), C1 ** -0.5, 0.4375),
        "outward_one": centred(seeds[7], (HID1, C1), HID1 ** -0.5, 0.21875),
        "gain_down": jnp.clip(1.0 + 0.15 * jax.random.normal(seeds[8], (C1,), jnp.float32), 0.25, 1.75).astype(jnp.bfloat16),
        "project_down": centred(seeds[9], (4 * C1, C2), (4 * C1) ** -0.5, 0.21875),
        "kernel_two": centred(seeds[10], (KSIZE, KSIZE, C2), (KSIZE * KSIZE) ** -0.5, 0.875),
        "gain_two": jnp.clip(1.0 + 0.15 * jax.random.normal(seeds[11], (C2,), jnp.float32), 0.25, 1.75).astype(jnp.bfloat16),
        "inward_two": centred(seeds[12], (C2, HID2), C2 ** -0.5, 0.3125),
        "outward_two": centred(seeds[13], (HID2, C2), HID2 ** -0.5, 0.15625),
    }


def depthwise(field, kernel):
    return lax.conv_general_dilated(field.astype(jnp.float32), kernel.astype(jnp.float32)[:, :, None, :], (1, 1), 'SAME', dimension_numbers=('NHWC', 'HWIO', 'NHWC'), feature_group_count=field.shape[-1], precision=lax.Precision.HIGHEST)

def layer_norm(values, gain):
    centre = lax.optimization_barrier(jnp.mean(values, axis=-1, keepdims=True))
    offset = values - centre
    spread = lax.optimization_barrier(jnp.mean(offset * offset, axis=-1, keepdims=True))
    return offset * lax.rsqrt(spread + 1e-06) * gain.astype(jnp.float32)

def gelu_exact(values):
    return jax.nn.gelu(values, approximate=False)

def slot_pass(tile_feats, cotangent, weights):
    kernel_one, gain_one, inward_one, outward_one, gain_down, project_down, kernel_two, gain_two, inward_two, outward_two = weights
    slot_count = tile_feats.shape[0]
    side_cells = tile_feats.shape[1]
    narrow_width = tile_feats.shape[3]
    half_side = side_cells // 2
    wide_width = project_down.shape[1]
    first_rows = slot_count * side_cells * side_cells
    second_rows = slot_count * half_side * half_side
    normed = layer_norm(depthwise(tile_feats, kernel_one), gain_one).astype(jnp.bfloat16).reshape(first_rows, narrow_width)
    expand = jnp.dot(normed, inward_one, preferred_element_type=jnp.float32)
    hidden = gelu_exact(expand).astype(jnp.bfloat16)
    flat_input = tile_feats.reshape(first_rows, narrow_width)
    section_one = (flat_input.astype(jnp.float32) + jnp.dot(hidden, outward_one, preferred_element_type=jnp.float32)).astype(jnp.bfloat16)
    down_normed = layer_norm(section_one.astype(jnp.float32), gain_down).astype(jnp.bfloat16)
    patches = down_normed.reshape(slot_count, half_side, 2, half_side, 2, narrow_width).transpose(0, 1, 3, 2, 4, 5).reshape(second_rows, 4 * narrow_width)
    merged = jnp.dot(patches, project_down, preferred_element_type=jnp.float32).astype(jnp.bfloat16)
    merged_grid = merged.reshape(slot_count, half_side, half_side, wide_width).astype(jnp.float32)

    def second_norm(values):
        return layer_norm(depthwise(values, kernel_two), gain_two)
    normed_two = second_norm(merged_grid).astype(jnp.bfloat16).reshape(second_rows, wide_width)
    expand_two = jnp.dot(normed_two, inward_two, preferred_element_type=jnp.float32)
    hidden_two = gelu_exact(expand_two).astype(jnp.bfloat16)
    features = (merged.astype(jnp.float32) + jnp.dot(hidden_two, outward_two, preferred_element_type=jnp.float32)).astype(jnp.bfloat16)
    flat_cot = cotangent.reshape(second_rows, wide_width)
    back_hidden_two = jnp.dot(flat_cot, outward_two.T, preferred_element_type=jnp.float32).astype(jnp.bfloat16)
    unused, gelu_back_two = jax.vjp(gelu_exact, expand_two)
    back_expand_two = gelu_back_two(back_hidden_two.astype(jnp.float32))[0].astype(jnp.bfloat16)
    back_normed_two = jnp.dot(back_expand_two, inward_two.T, preferred_element_type=jnp.float32).astype(jnp.bfloat16)
    unused, norm_back_two = jax.vjp(second_norm, merged_grid)
    back_depth = norm_back_two(back_normed_two.astype(jnp.float32).reshape(slot_count, half_side, half_side, wide_width))[0]
    back_merged = (flat_cot.astype(jnp.float32) + back_depth.reshape(second_rows, wide_width)).astype(jnp.bfloat16)
    grad_project = jnp.dot(patches.T, back_merged, preferred_element_type=jnp.float32)
    back_patches = jnp.dot(back_merged, project_down.T, preferred_element_type=jnp.float32).astype(jnp.bfloat16)
    back_down = back_patches.reshape(slot_count, half_side, half_side, 2, 2, narrow_width).transpose(0, 1, 3, 2, 4, 5).reshape(first_rows, narrow_width)
    unused, norm_back_down = jax.vjp(lambda values: layer_norm(values, gain_down), section_one.astype(jnp.float32))
    back_section = norm_back_down(back_down.astype(jnp.float32))[0].astype(jnp.bfloat16)
    grad_outward = jnp.dot(hidden.T, back_section, preferred_element_type=jnp.float32)
    back_hidden = jnp.dot(back_section, outward_one.T, preferred_element_type=jnp.float32).astype(jnp.bfloat16)
    unused, gelu_back = jax.vjp(gelu_exact, expand)
    back_expand = gelu_back(back_hidden.astype(jnp.float32))[0].astype(jnp.bfloat16)
    grad_inward = jnp.dot(normed.T, back_expand, preferred_element_type=jnp.float32)
    return (features.reshape(slot_count, half_side, half_side, wide_width), grad_inward, grad_outward, grad_project)

def column_mask(mask, rank):
    return mask.reshape(mask.shape + (1,) * rank)

def fill_slots(own_rows, partner_rows, own_number, partner_number):
    capacity = own_rows.shape[0]
    slot_index = jnp.arange(capacity, dtype=jnp.int32)
    take_own = slot_index < own_number
    shifted = jnp.clip(slot_index - own_number, 0, capacity - 1)
    take_partner = jnp.logical_and(slot_index >= own_number, slot_index - own_number < partner_number)
    rank = own_rows.ndim - 1
    zero_value = jnp.zeros((), own_rows.dtype)
    return jnp.where(column_mask(take_own, rank), own_rows, jnp.where(column_mask(take_partner, rank), partner_rows[shifted], zero_value))

def reference(tile_feats, cotangent, keep_list, tile_plan, kernel_one, gain_one, inward_one, outward_one, gain_down, project_down, kernel_two, gain_two, inward_two, outward_two):
    weights = (kernel_one, gain_one, inward_one, outward_one, gain_down, project_down, kernel_two, gain_two, inward_two, outward_two)
    group_total = keep_list.shape[0]
    candidates = keep_list.shape[1]
    capacity = candidates // 2
    side_cells = tile_feats.shape[1]
    narrow_width = tile_feats.shape[3]
    half_side = cotangent.shape[1]
    wide_width = cotangent.shape[3]
    tile_blocks = tile_feats.reshape(group_total, candidates, side_cells, side_cells, narrow_width)
    cot_blocks = cotangent.reshape(group_total, candidates, half_side, half_side, wide_width)
    counts = tile_plan[:, 0]
    partner_bits = tile_plan[:, 1]
    positions = jnp.arange(candidates, dtype=jnp.int32)
    live = positions[None, :] < counts[:, None]
    zero_value = jnp.zeros((), jnp.bfloat16)
    ordered_tiles = jnp.where(column_mask(live, 3), jax.vmap(lambda block_rows, ordering: block_rows[ordering])(tile_blocks, keep_list), zero_value)
    ordered_cot = jnp.where(column_mask(live, 3), jax.vmap(lambda block_rows, ordering: block_rows[ordering])(cot_blocks, keep_list), zero_value)
    group_index = jnp.arange(group_total, dtype=jnp.int32)
    slide_index = group_index // REPLICAS
    replica = group_index % REPLICAS
    partner = jnp.bitwise_xor(slide_index, jnp.left_shift(jnp.ones_like(partner_bits), partner_bits)) * REPLICAS + replica
    own_numbers = jnp.minimum(counts, capacity)
    extra_numbers = jnp.clip(counts - capacity, 0, capacity)

    def step(totals, group):
        partner_group = partner[group]
        slot_tiles = fill_slots(ordered_tiles[group, :capacity], ordered_tiles[partner_group, capacity:], own_numbers[group], extra_numbers[partner_group])
        slot_cot = fill_slots(ordered_cot[group, :capacity], ordered_cot[partner_group, capacity:], own_numbers[group], extra_numbers[partner_group])
        outcome = slot_pass(slot_tiles, slot_cot, weights)
        return ((totals[0] + outcome[1], totals[1] + outcome[2], totals[2] + outcome[3]), outcome[0])
    start = (jnp.zeros(inward_one.shape, jnp.float32), jnp.zeros(outward_one.shape, jnp.float32), jnp.zeros(project_down.shape, jnp.float32))
    totals, slot_feats = lax.scan(step, start, group_index)
    returned_index = jnp.clip(own_numbers[partner][:, None] + positions[None, :capacity], 0, capacity - 1)
    returned = slot_feats[partner[:, None], returned_index]
    position_feats = jnp.concatenate([slot_feats, returned], axis=1)
    place = lax.optimization_barrier(jnp.sum(jnp.where(keep_list[:, None, :] == positions[None, :, None], positions[None, None, :], 0), axis=2)).astype(jnp.int32)
    chosen = jax.vmap(lambda block_rows, where_at: block_rows[where_at])(position_feats, place)
    features = jnp.where(column_mask(place < counts[:, None], 3), chosen, zero_value).reshape(cotangent.shape)
    return (features, totals[0], totals[1], totals[2])
```

```python
import jax
import jax.numpy as jnp
from jax import lax
from jax.sharding import Mesh
from jax.sharding import PartitionSpec as P

SLIDE = ("x", "z_high", "z_low", "core")
SLIDE_REP = ("x", "z_high", "z_low", "core", "rep")


def exchange(pieces, axis):
    return lax.all_to_all(pieces, axis, split_axis=0, concat_axis=0, tiled=True)


def summed(pieces, axis):
    return exchange(pieces, axis).astype(jnp.float32).sum(axis=0)


def scatter_sum(stacked):
    width = stacked.shape[-1]
    part = summed(stacked, "core").astype(jnp.bfloat16)
    part = summed(part.reshape(4, part.shape[0] // 4, width), "x").astype(jnp.bfloat16)
    part = summed(part.reshape(4, part.shape[0] // 4, width), "z_low").astype(jnp.bfloat16)
    part = summed(part.reshape(4, part.shape[0] // 4, width), "z_high")
    return summed(jnp.broadcast_to(part, (4, *part.shape)), "rep")


def regrouping(hidden):
    share = hidden // 128
    row = jnp.arange(hidden, dtype=jnp.int32)
    slot, slide = row % share, row // share
    core, z, x = slide % 2, slide // 2 % 16, slide // 32
    order = ((core * 4 + x) * 4 + z % 4) * 4 + z // 4
    target = order * share + slot
    return (target[:, None] == row[None, :]).astype(jnp.bfloat16)


def regrouped(values, placing):
    return jnp.dot(values, placing, preferred_element_type=jnp.float32).astype(jnp.bfloat16)


def depthwise(field, kernel):
    return lax.conv_general_dilated(
        field.astype(jnp.float32),
        kernel.astype(jnp.float32)[:, :, None, :],
        (1, 1),
        "SAME",
        dimension_numbers=("NHWC", "HWIO", "NHWC"),
        feature_group_count=field.shape[-1],
        precision=lax.Precision.HIGHEST,
    )


def layer_norm(values, gain):
    centre = jnp.mean(values, axis=-1, keepdims=True)
    offset = values - centre
    spread = jnp.mean(offset * offset, axis=-1, keepdims=True)
    return offset * lax.rsqrt(spread + 1e-06) * gain.astype(jnp.float32)


def gelu_exact(values):
    return jax.nn.gelu(values, approximate=False)


def slot_pass(tile_feats, cotangent, weights):
    (
        kernel_one,
        gain_one,
        inward_one,
        outward_one,
        gain_down,
        project_down,
        kernel_two,
        gain_two,
        inward_two,
        outward_two,
    ) = weights
    placing = regrouping(inward_one.shape[1])
    inward_one = regrouped(inward_one, placing)
    outward_one = jnp.dot(placing.T, outward_one, preferred_element_type=jnp.float32).astype(
        jnp.bfloat16
    )
    slot_count = tile_feats.shape[0]
    side_cells = tile_feats.shape[1]
    narrow_width = tile_feats.shape[3]
    half_side = side_cells // 2
    wide_width = project_down.shape[1]
    first_rows = slot_count * side_cells * side_cells
    second_rows = slot_count * half_side * half_side
    normed = (
        layer_norm(depthwise(tile_feats, kernel_one), gain_one)
        .astype(jnp.bfloat16)
        .reshape(first_rows, narrow_width)
    )
    expand = jnp.dot(normed, inward_one, preferred_element_type=jnp.float32)
    hidden = gelu_exact(expand).astype(jnp.bfloat16)
    flat_input = tile_feats.reshape(first_rows, narrow_width)
    section_one = (
        flat_input.astype(jnp.float32)
        + jnp.dot(hidden, outward_one, preferred_element_type=jnp.float32)
    ).astype(jnp.bfloat16)
    down_normed = layer_norm(section_one.astype(jnp.float32), gain_down).astype(jnp.bfloat16)
    patches = (
        down_normed.reshape(slot_count, half_side, 2, half_side, 2, narrow_width)
        .transpose(0, 1, 3, 2, 4, 5)
        .reshape(second_rows, 4 * narrow_width)
    )
    merged = jnp.dot(patches, project_down, preferred_element_type=jnp.float32).astype(jnp.bfloat16)
    merged_grid = merged.reshape(slot_count, half_side, half_side, wide_width).astype(jnp.float32)

    def second_norm(values):
        return layer_norm(depthwise(values, kernel_two), gain_two)

    normed_two = second_norm(merged_grid).astype(jnp.bfloat16).reshape(second_rows, wide_width)
    expand_two = jnp.dot(normed_two, inward_two, preferred_element_type=jnp.float32)
    hidden_two = gelu_exact(expand_two).astype(jnp.bfloat16)
    features = (
        merged.astype(jnp.float32)
        + jnp.dot(hidden_two, outward_two, preferred_element_type=jnp.float32)
    ).astype(jnp.bfloat16)
    flat_cot = cotangent.reshape(second_rows, wide_width)
    back_hidden_two = jnp.dot(flat_cot, outward_two.T, preferred_element_type=jnp.float32).astype(
        jnp.bfloat16
    )
    unused, gelu_back_two = jax.vjp(gelu_exact, expand_two)
    back_expand_two = gelu_back_two(back_hidden_two.astype(jnp.float32))[0].astype(jnp.bfloat16)
    back_normed_two = jnp.dot(
        back_expand_two, inward_two.T, preferred_element_type=jnp.float32
    ).astype(jnp.bfloat16)
    unused, norm_back_two = jax.vjp(second_norm, merged_grid)
    back_depth = norm_back_two(
        back_normed_two.astype(jnp.float32).reshape(slot_count, half_side, half_side, wide_width)
    )[0]
    back_merged = (
        flat_cot.astype(jnp.float32) + back_depth.reshape(second_rows, wide_width)
    ).astype(jnp.bfloat16)
    grad_project = jnp.dot(
        regrouped(patches, placing).T, back_merged, preferred_element_type=jnp.float32
    )
    back_patches = jnp.dot(back_merged, project_down.T, preferred_element_type=jnp.float32).astype(
        jnp.bfloat16
    )
    back_down = (
        back_patches.reshape(slot_count, half_side, half_side, 2, 2, narrow_width)
        .transpose(0, 1, 3, 2, 4, 5)
        .reshape(first_rows, narrow_width)
    )
    unused, norm_back_down = jax.vjp(
        lambda values: layer_norm(values, gain_down), section_one.astype(jnp.float32)
    )
    back_section = norm_back_down(back_down.astype(jnp.float32))[0].astype(jnp.bfloat16)
    grad_outward = jnp.dot(hidden.T, back_section, preferred_element_type=jnp.float32)
    back_hidden = jnp.dot(back_section, outward_one.T, preferred_element_type=jnp.float32).astype(
        jnp.bfloat16
    )
    unused, gelu_back = jax.vjp(gelu_exact, expand)
    back_expand = gelu_back(back_hidden.astype(jnp.float32))[0].astype(jnp.bfloat16)
    grad_inward = jnp.dot(back_expand.T, normed, preferred_element_type=jnp.float32)
    return (
        features.reshape(slot_count, half_side, half_side, wide_width),
        grad_inward,
        grad_outward,
        grad_project,
    )


def column_mask(mask, rank):
    return mask.reshape(mask.shape + (1,) * rank)


def per_device(
    tile_feats,
    cotangent,
    keep_list,
    tile_plan,
    kernel_one,
    gain_one,
    inward_one,
    outward_one,
    gain_down,
    project_down,
    kernel_two,
    gain_two,
    inward_two,
    outward_two,
):
    weights = (
        kernel_one,
        gain_one,
        inward_one,
        outward_one,
        gain_down,
        project_down,
        kernel_two,
        gain_two,
        inward_two,
        outward_two,
    )
    candidates = tile_feats.shape[0]
    positions = jnp.arange(candidates, dtype=jnp.int32)
    kept = jnp.logical_and(
        keep_list[0][None, :] == positions[:, None], positions[None, :] < tile_plan[0, 0]
    ).any(axis=1)
    zero_value = jnp.zeros((), jnp.bfloat16)
    own_tiles = jnp.where(column_mask(kept, 3), tile_feats, zero_value)
    own_cot = jnp.where(column_mask(kept, 3), cotangent, zero_value)
    tile_features, grad_inward, grad_outward, grad_project = slot_pass(own_tiles, own_cot, weights)
    features = jnp.where(column_mask(kept, 3), tile_features, zero_value)
    stacked = jnp.concatenate([grad_inward, grad_outward, grad_project], axis=1)
    rows, width = stacked.shape
    share = scatter_sum(stacked.astype(jnp.bfloat16).reshape(2, rows // 2, width))
    narrow = grad_inward.shape[1]
    return (features, share[:, :narrow].T, share[:, narrow : 2 * narrow], share[:, 2 * narrow :])


def solution(mesh):
    split = Mesh(mesh.devices.reshape(4, 4, 4, 2, mesh.shape["rep"]), SLIDE_REP)
    return jax.shard_map(
        per_device,
        mesh=split,
        in_specs=(
            P(SLIDE_REP, None, None, None),
            P(SLIDE_REP, None, None, None),
            P(SLIDE_REP, None),
            P(SLIDE_REP, None),
            P(),
            P(),
            P(),
            P(),
            P(),
            P(),
            P(),
            P(),
            P(),
            P(),
        ),
        out_specs=(P(SLIDE_REP, None, None, None), P(None, SLIDE), P(SLIDE, None), P(SLIDE, None)),
        check_vma=False,
    )
```

```python
import jax
import jax.numpy as jnp
from jax import lax
from jax.experimental import pallas as pl
from jax.experimental.pallas import tpu as pltpu
from jax.sharding import Mesh
from jax.sharding import PartitionSpec as P

SLIDE = ("x", "z", "core")
SLIDE_REP = ("x", "z", "core", "rep")
F32 = jnp.float32
BF16 = jnp.bfloat16
TILES = 4
CELLS = 16
NARROW = 192
WIDE = 384
HIDDEN = 768
HIDDEN_TWO = 1536
ROWS = 256
ROWS_TWO = 64
HALF_ROOT = 0.7071067811865476
DENSITY = 0.3989422804014327


def product(left, right, contract=(1, 0)):
    return lax.dot_general(
        left, right, (((contract[0],), (contract[1],)), ((), ())), preferred_element_type=F32
    )


def statistics(values, eps=1e-6):
    offset = values - jnp.mean(values, axis=-1, keepdims=True)
    scale = lax.rsqrt(jnp.mean(offset * offset, axis=-1, keepdims=True) + eps)
    return offset * scale, scale


def norm_back(scaled, scale, gained):
    mean = jnp.mean(gained, axis=-1, keepdims=True)
    along = jnp.mean(gained * scaled, axis=-1, keepdims=True)
    return scale * (gained - mean - scaled * along)


def gelu_parts(values):
    below = 0.5 + 0.5 * lax.erf(values * HALF_ROOT)
    return values * below, below + values * (DENSITY * jnp.exp(-0.5 * values * values))


def gelu_rows(expand_ref, hidden_ref, block):
    def step(index, carry):
        rows = pl.ds(pl.multiple_of(index * block, block), block)
        hidden, slope = gelu_parts(expand_ref[rows, :])
        hidden_ref[rows, :] = hidden.astype(BF16)
        expand_ref[rows, :] = slope
        return carry

    lax.fori_loop(0, expand_ref.shape[0] // block, step, 0)


def slope_rows(slope_ref, back_ref, block):
    def step(index, carry):
        rows = pl.ds(pl.multiple_of(index * block, block), block)
        back_ref[rows, :] = (slope_ref[rows, :] * back_ref[rows, :].astype(F32)).astype(BF16)
        return carry

    lax.fori_loop(0, slope_ref.shape[0] // block, step, 0)


def one_hot(shape, source, source_dim):
    own = lax.broadcasted_iota(jnp.int32, shape, 1 - source_dim)
    index = lax.broadcasted_iota(jnp.int32, shape, source_dim)
    return jnp.where(own == source(index), 1.0, 0.0).astype(BF16)


def hidden_source(place):
    third, rest = place >> 8, place & 255
    core, pair, low = rest >> 7, (rest >> 1) & 63, rest & 1
    return (pair * 2 + core) * 6 + third * 2 + low


def row_source(place):
    tile, x, y = place & 3, (place >> 2) & 3, (place >> 4) & 3
    column, row = (place >> 6) & 1, place >> 7
    return tile * 64 + (2 * y + row) * 8 + 2 * x + column


def cell_source(place):
    return (place & 3) * 16 + (place >> 2)


def tile_place(place):
    return (place & 15) * 4 + (place >> 4)


def conv_one(tile, kernel_ref):
    cell = lax.broadcasted_iota(jnp.int32, (8, NARROW), 0)
    sums = [None] * 8
    for dx in range(-3, 4):
        inside = jnp.logical_and(cell + dx >= 0, cell + dx < 8)
        taps = [jnp.broadcast_to(kernel_ref[dy, dx + 3 : dx + 4, :], (8, NARROW)) for dy in range(7)]
        for source in range(8):
            line = tile[source]
            if dx != 0:
                line = jnp.where(inside, pltpu.roll(line, (-dx) % 8, 0), 0.0)
            for target in range(max(0, source - 3), min(8, source + 4)):
                term = taps[source - target + 3] * line
                sums[target] = term if sums[target] is None else sums[target] + term
    return jnp.concatenate(sums, axis=0)


def conv_two(source_ref, kernel_ref, out_ref, back):
    for part in range(WIDE // 128):
        lanes = slice(part * 128, part * 128 + 128)
        cells = [source_ref[4 * c : 4 * c + 8, lanes] for c in range(CELLS)]
        taps = {}
        for dy in range(7):
            for dx in range(7):
                taps[dy, dx] = jnp.broadcast_to(kernel_ref[dy, dx : dx + 1, lanes], (8, 128))
        for y in range(4):
            for x in range(4):
                total = None
                for fy in range(4):
                    for fx in range(4):
                        dy, dx = (y - fy, x - fx) if back else (fy - y, fx - x)
                        term = taps[dy + 3, dx + 3] * cells[fy * 4 + fx]
                        total = term if total is None else total + term
                place = 4 * (y * 4 + x)
                out_ref[place : place + 4, lanes] = total[0:4]


def step_kernel(
    keep_ref,
    plan_ref,
    feats_ref,
    cot_ref,
    kernel_one_ref,
    gain_one_ref,
    inward_one_ref,
    outward_one_ref,
    gain_down_ref,
    project_ref,
    kernel_two_ref,
    gain_two_ref,
    inward_two_ref,
    outward_two_ref,
    features_ref,
    grads_ref,
    taps_one,
    taps_two,
    field,
    normed_rows,
    expand,
    hidden,
    back_hidden,
    expand_two,
    hidden_two,
    back_two,
    padded,
    spread,
):
    count = plan_ref[0, 0]
    kept = []
    for tile in range(TILES):
        place = jnp.int32(0)
        for position in range(TILES):
            place = place + jnp.where(keep_ref[0, position] == tile, position, 0)
        kept.append(place < count)
    taps_one[...] = kernel_one_ref[...].astype(F32)
    taps_two[...] = kernel_two_ref[...].astype(F32)
    gain_one = gain_one_ref[...].astype(F32)
    gain_down = gain_down_ref[...].astype(F32)
    gain_two = gain_two_ref[...].astype(F32)

    placing = one_hot((HIDDEN, HIDDEN), hidden_source, 1)
    inward = product(inward_one_ref[...], placing).astype(BF16)
    outward = product(outward_one_ref[...], placing).astype(BF16)

    for tile in range(TILES):
        own = jnp.where(kept[tile], feats_ref[tile].astype(F32), 0.0)
        rows = slice(tile * 64, tile * 64 + 64)
        field[rows, :] = own.reshape(64, NARROW).astype(BF16)
        scaled, _ = statistics(conv_one(own, taps_one))
        normed_rows[rows, :] = (scaled * gain_one).astype(BF16)

    gather_rows = one_hot((ROWS, ROWS), row_source, 0)
    normed = product(gather_rows, normed_rows[...]).astype(BF16)
    field_rows = product(gather_rows, field[...])
    expand[...] = product(normed, inward)
    gelu_rows(expand, hidden, 16)
    section = (field_rows + product(hidden[...], outward, (1, 1))).astype(BF16).astype(F32)
    scaled_down, scale_down = statistics(section)
    down = (scaled_down * gain_down).astype(BF16)
    merged = None
    for block in range(4):
        part = product(
            down[block * 64 : block * 64 + 64], project_ref[block * NARROW : (block + 1) * NARROW, :]
        )
        merged = part if merged is None else merged + part
    merged = merged.astype(BF16).astype(F32)

    padded[0:ROWS_TWO, :] = merged
    padded[ROWS_TWO : ROWS_TWO + 8, :] = jnp.zeros((8, WIDE), F32)
    conv_two(padded, taps_two, spread, False)
    scaled_two, scale_two = statistics(spread[...])
    normed_two = (scaled_two * gain_two).astype(BF16)
    expand_two[...] = product(normed_two, inward_two_ref[...])
    gelu_rows(expand_two, hidden_two, 16)
    features = (merged + product(hidden_two[...], outward_two_ref[...])).astype(BF16)
    scatter_cells = one_hot((ROWS_TWO, ROWS_TWO), tile_place, 0)
    spread[...] = product(scatter_cells, features)
    for index in range(CELLS):
        tile, y = index // 4, index % 4
        own = spread[4 * index : 4 * index + 4, :]
        features_ref[tile, y] = jnp.where(kept[tile], own, 0.0).astype(BF16)

    for index in range(CELLS):
        tile, y = index // 4, index % 4
        own = jnp.where(kept[tile], cot_ref[tile, y].astype(F32), 0.0)
        spread[4 * index : 4 * index + 4, :] = own
    gather_cells = one_hot((ROWS_TWO, ROWS_TWO), cell_source, 0)
    flat_cot = product(gather_cells, spread[...].astype(BF16))
    back_two[...] = product(flat_cot.astype(BF16), outward_two_ref[...], (1, 1)).astype(BF16)
    slope_rows(expand_two, back_two, 16)
    back_normed_two = product(back_two[...], inward_two_ref[...], (1, 1)).astype(BF16).astype(F32)
    padded[0:ROWS_TWO, :] = norm_back(scaled_two, scale_two, back_normed_two * gain_two)
    conv_two(padded, taps_two, spread, True)
    back_merged = (flat_cot + spread[...]).astype(BF16)

    patches = None
    back_down = []
    for block in range(4):
        rows = slice(block * NARROW, (block + 1) * NARROW)
        part = product(down[block * 64 : block * 64 + 64], placing[rows, :])
        patches = part if patches is None else patches + part
        back_down.append(product(back_merged, project_ref[rows, :], (1, 1)))
    back_down = jnp.concatenate(back_down, axis=0).astype(BF16).astype(F32)
    grad_project = product(patches.astype(BF16), back_merged, (0, 0)).astype(BF16)
    back_section = norm_back(scaled_down, scale_down, back_down * gain_down).astype(BF16)
    back_hidden[...] = product(back_section, outward).astype(BF16)
    slope_rows(expand, back_hidden, 16)
    grad_outward = product(hidden[...], back_section, (0, 0)).astype(BF16)
    grad_inward = product(back_hidden[...], normed, (0, 0)).astype(BF16)
    for third in range(3):
        for core in range(2):
            rows = slice(third * 256 + core * 128, third * 256 + core * 128 + 128)
            left = third * HIDDEN
            grads_ref[core, :, left : left + NARROW] = grad_inward[rows]
            grads_ref[core, :, left + NARROW : left + WIDE] = grad_outward[rows]
            grads_ref[core, :, left + WIDE : left + HIDDEN] = grad_project[rows]


def local_step(*operands):
    smem = pl.BlockSpec(memory_space=pltpu.SMEM)
    vmem = pl.BlockSpec(memory_space=pltpu.VMEM)
    return pl.pallas_call(
        step_kernel,
        in_specs=[smem, smem] + [vmem] * 12,
        out_specs=[vmem, vmem],
        out_shape=[
            jax.ShapeDtypeStruct((TILES, 4, 4, WIDE), BF16),
            jax.ShapeDtypeStruct((2, 128, 3 * HIDDEN), BF16),
        ],
        scratch_shapes=[
            pltpu.VMEM((7, 7, NARROW), F32),
            pltpu.VMEM((7, 7, WIDE), F32),
            pltpu.VMEM((ROWS, NARROW), BF16),
            pltpu.VMEM((ROWS, NARROW), BF16),
            pltpu.VMEM((ROWS, HIDDEN), F32),
            pltpu.VMEM((ROWS, HIDDEN), BF16),
            pltpu.VMEM((ROWS, HIDDEN), BF16),
            pltpu.VMEM((ROWS_TWO, HIDDEN_TWO), F32),
            pltpu.VMEM((ROWS_TWO, HIDDEN_TWO), BF16),
            pltpu.VMEM((ROWS_TWO, HIDDEN_TWO), BF16),
            pltpu.VMEM((ROWS_TWO + 8, WIDE), F32),
            pltpu.VMEM((ROWS_TWO, WIDE), F32),
        ],
        name="local_step",
    )(*operands)


def pair_kernel(parts_ref, out_ref):
    def step(index, carry):
        rows = pl.ds(pl.multiple_of(index * 16, 16), 16)
        total = parts_ref[0, rows, :].astype(F32) + parts_ref[1, rows, :].astype(F32)
        for slide in range(8):
            out_ref[index * 8 + slide] = total[2 * slide : 2 * slide + 2].astype(BF16)
        return carry

    lax.fori_loop(0, parts_ref.shape[1] // 16, step, 0)


def pair_sum(parts):
    vmem = pl.BlockSpec(memory_space=pltpu.VMEM)
    return pl.pallas_call(
        pair_kernel,
        in_specs=[vmem],
        out_specs=vmem,
        out_shape=jax.ShapeDtypeStruct((64, 2, parts.shape[2]), BF16),
        name="pair_sum",
    )(parts)


def exchange(pieces, axis):
    return lax.all_to_all(pieces, axis, split_axis=0, concat_axis=0, tiled=True)


def per_device(
    tile_feats,
    cotangent,
    keep_list,
    tile_plan,
    kernel_one,
    gain_one,
    inward_one,
    outward_one,
    gain_down,
    project_down,
    kernel_two,
    gain_two,
    inward_two,
    outward_two,
):
    features, grads = local_step(
        keep_list,
        tile_plan,
        tile_feats,
        cotangent,
        kernel_one,
        gain_one.reshape(1, NARROW),
        inward_one,
        outward_one.T,
        gain_down.reshape(1, NARROW),
        project_down,
        kernel_two,
        gain_two.reshape(1, WIDE),
        inward_two,
        outward_two,
    )
    own = pair_sum(exchange(grads, "core"))
    own = exchange(own, ("x", "z")).astype(F32).sum(axis=0)
    share = exchange(jnp.broadcast_to(own, (4, *own.shape)), "rep").sum(axis=0)
    share = share.reshape(2, 3, HIDDEN).transpose(1, 0, 2).reshape(6, HIDDEN)
    return (features, share[:, :NARROW].T, share[:, NARROW:WIDE], share[:, WIDE:])


def solution(mesh):
    split = Mesh(mesh.devices.reshape(4, 16, 2, mesh.shape["rep"]), SLIDE_REP)
    return jax.shard_map(
        per_device,
        mesh=split,
        in_specs=(
            P(SLIDE_REP, None, None, None),
            P(SLIDE_REP, None, None, None),
            P(SLIDE_REP, None),
            P(SLIDE_REP, None),
            P(),
            P(),
            P(),
            P(),
            P(),
            P(),
            P(),
            P(),
            P(),
            P(),
        ),
        out_specs=(P(SLIDE_REP, None, None, None), P(None, SLIDE), P(SLIDE, None), P(SLIDE, None)),
        check_vma=False,
    )
```

```python
import jax
import jax.numpy as jnp
from jax import lax
from jax.experimental import pallas as pl
from jax.experimental.pallas import tpu as pltpu
from jax.sharding import Mesh
from jax.sharding import PartitionSpec as P

SLIDE = ("x", "z", "core")
SLIDE_REP = ("x", "z", "core", "rep")
F32 = jnp.float32
BF16 = jnp.bfloat16
TILES = 4
CELLS = 16
NARROW = 192
WIDE = 384
HIDDEN = 768
HIDDEN_TWO = 1536
ROWS = 256
ROWS_TWO = 64
HALF_ROOT = 0.7071067811865476
DENSITY = 0.3989422804014327


def product(left, right, contract=(1, 0)):
    return lax.dot_general(
        left, right, (((contract[0],), (contract[1],)), ((), ())), preferred_element_type=F32
    )


def statistics(values, eps=1e-6):
    offset = values - jnp.mean(values, axis=-1, keepdims=True)
    scale = lax.rsqrt(jnp.mean(offset * offset, axis=-1, keepdims=True) + eps)
    return offset * scale, scale


def norm_back(scaled, scale, gained):
    mean = jnp.mean(gained, axis=-1, keepdims=True)
    along = jnp.mean(gained * scaled, axis=-1, keepdims=True)
    return scale * (gained - mean - scaled * along)


def gelu_parts(values):
    below = 0.5 + 0.5 * lax.erf(values * HALF_ROOT)
    return values * below, below + values * (DENSITY * jnp.exp(-0.5 * values * values))


def gelu_rows(expand_ref, hidden_ref, block):
    def step(index, carry):
        rows = pl.ds(pl.multiple_of(index * block, block), block)
        hidden, slope = gelu_parts(expand_ref[rows, :])
        hidden_ref[rows, :] = hidden.astype(BF16)
        expand_ref[rows, :] = slope
        return carry

    lax.fori_loop(0, expand_ref.shape[0] // block, step, 0)


def slope_rows(slope_ref, back_ref, block):
    def step(index, carry):
        rows = pl.ds(pl.multiple_of(index * block, block), block)
        back_ref[rows, :] = (slope_ref[rows, :] * back_ref[rows, :].astype(F32)).astype(BF16)
        return carry

    lax.fori_loop(0, slope_ref.shape[0] // block, step, 0)


def one_hot(shape, source, source_dim):
    own = lax.broadcasted_iota(jnp.int32, shape, 1 - source_dim)
    index = lax.broadcasted_iota(jnp.int32, shape, source_dim)
    return jnp.where(own == source(index), 1.0, 0.0).astype(BF16)


def hidden_source(place):
    third, rest = place >> 8, place & 255
    core, pair, low = rest >> 7, (rest >> 1) & 63, rest & 1
    return (pair * 2 + core) * 6 + third * 2 + low


def row_source(place):
    tile, x, y = place & 3, (place >> 2) & 3, (place >> 4) & 3
    column, row = (place >> 6) & 1, place >> 7
    return tile * 64 + (2 * y + row) * 8 + 2 * x + column


def cell_source(place):
    return (place & 3) * 16 + (place >> 2)


def tile_place(place):
    return (place & 15) * 4 + (place >> 4)


def conv_one(tile, kernel_ref):
    cell = lax.broadcasted_iota(jnp.int32, (8, NARROW), 0)
    sums = [None] * 8
    for dx in range(-3, 4):
        inside = jnp.logical_and(cell + dx >= 0, cell + dx < 8)
        taps = [jnp.broadcast_to(kernel_ref[dy, dx + 3 : dx + 4, :], (8, NARROW)) for dy in range(7)]
        for source in range(8):
            line = tile[source]
            if dx != 0:
                line = jnp.where(inside, pltpu.roll(line, (-dx) % 8, 0), 0.0)
            for target in range(max(0, source - 3), min(8, source + 4)):
                term = taps[source - target + 3] * line
                sums[target] = term if sums[target] is None else sums[target] + term
    return jnp.concatenate(sums, axis=0)


def conv_two(source_ref, kernel_ref, out_ref, back):
    for part in range(WIDE // 128):
        lanes = slice(part * 128, part * 128 + 128)
        cells = [source_ref[4 * c : 4 * c + 8, lanes] for c in range(CELLS)]
        taps = {}
        for dy in range(7):
            for dx in range(7):
                taps[dy, dx] = jnp.broadcast_to(kernel_ref[dy, dx : dx + 1, lanes], (8, 128))
        for y in range(4):
            for x in range(4):
                total = None
                for fy in range(4):
                    for fx in range(4):
                        dy, dx = (y - fy, x - fx) if back else (fy - y, fx - x)
                        term = taps[dy + 3, dx + 3] * cells[fy * 4 + fx]
                        total = term if total is None else total + term
                place = 4 * (y * 4 + x)
                out_ref[place : place + 4, lanes] = total[0:4]


def step_kernel(
    keep_ref,
    plan_ref,
    feats_ref,
    cot_ref,
    kernel_one_ref,
    gain_one_ref,
    inward_one_ref,
    outward_one_ref,
    gain_down_ref,
    project_ref,
    kernel_two_ref,
    gain_two_ref,
    inward_two_ref,
    outward_two_ref,
    features_ref,
    grads_ref,
    taps_one,
    taps_two,
    field,
    normed_rows,
    expand,
    hidden,
    back_hidden,
    expand_two,
    hidden_two,
    back_two,
    padded,
    spread,
):
    count = plan_ref[0, 0]
    kept = []
    for tile in range(TILES):
        place = jnp.int32(0)
        for position in range(TILES):
            place = place + jnp.where(keep_ref[0, position] == tile, position, 0)
        kept.append(place < count)
    taps_one[...] = kernel_one_ref[...].astype(F32)
    taps_two[...] = kernel_two_ref[...].astype(F32)
    gain_one = gain_one_ref[...].astype(F32).reshape(1, NARROW)
    gain_down = gain_down_ref[...].astype(F32).reshape(1, NARROW)
    gain_two = gain_two_ref[...].astype(F32).reshape(1, WIDE)

    placing = one_hot((HIDDEN, HIDDEN), hidden_source, 1)
    inward = product(inward_one_ref[...], placing).astype(BF16)
    outward = product(outward_one_ref[...], placing).astype(BF16)

    for tile in range(TILES):
        own = jnp.where(kept[tile], feats_ref[tile].astype(F32), 0.0)
        rows = slice(tile * 64, tile * 64 + 64)
        field[rows, :] = own.reshape(64, NARROW).astype(BF16)
        scaled, _ = statistics(conv_one(own, taps_one))
        normed_rows[rows, :] = (scaled * gain_one).astype(BF16)

    gather_rows = one_hot((ROWS, ROWS), row_source, 0)
    normed = product(gather_rows, normed_rows[...]).astype(BF16)
    field_rows = product(gather_rows, field[...])
    expand[...] = product(normed, inward)
    gelu_rows(expand, hidden, 16)
    section = (field_rows + product(hidden[...], outward, (1, 1))).astype(BF16).astype(F32)
    scaled_down, scale_down = statistics(section)
    down = (scaled_down * gain_down).astype(BF16)
    merged = None
    for block in range(4):
        part = product(
            down[block * 64 : block * 64 + 64], project_ref[block * NARROW : (block + 1) * NARROW, :]
        )
        merged = part if merged is None else merged + part
    merged = merged.astype(BF16).astype(F32)

    padded[0:ROWS_TWO, :] = merged
    padded[ROWS_TWO : ROWS_TWO + 8, :] = jnp.zeros((8, WIDE), F32)
    conv_two(padded, taps_two, spread, False)
    scaled_two, scale_two = statistics(spread[...])
    normed_two = (scaled_two * gain_two).astype(BF16)
    expand_two[...] = product(normed_two, inward_two_ref[...])
    gelu_rows(expand_two, hidden_two, 16)
    features = (merged + product(hidden_two[...], outward_two_ref[...])).astype(BF16)
    scatter_cells = one_hot((ROWS_TWO, ROWS_TWO), tile_place, 0)
    spread[...] = product(scatter_cells, features)
    for index in range(CELLS):
        tile, y = index // 4, index % 4
        own = spread[4 * index : 4 * index + 4, :]
        features_ref[tile, y] = jnp.where(kept[tile], own, 0.0).astype(BF16)

    for index in range(CELLS):
        tile, y = index // 4, index % 4
        own = jnp.where(kept[tile], cot_ref[tile, y].astype(F32), 0.0)
        spread[4 * index : 4 * index + 4, :] = own
    gather_cells = one_hot((ROWS_TWO, ROWS_TWO), cell_source, 0)
    flat_cot = product(gather_cells, spread[...].astype(BF16))
    back_two[...] = product(flat_cot.astype(BF16), outward_two_ref[...], (1, 1)).astype(BF16)
    slope_rows(expand_two, back_two, 16)
    back_normed_two = product(back_two[...], inward_two_ref[...], (1, 1)).astype(BF16).astype(F32)
    padded[0:ROWS_TWO, :] = norm_back(scaled_two, scale_two, back_normed_two * gain_two)
    conv_two(padded, taps_two, spread, True)
    back_merged = (flat_cot + spread[...]).astype(BF16)

    patches = None
    back_down = []
    for block in range(4):
        rows = slice(block * NARROW, (block + 1) * NARROW)
        part = product(down[block * 64 : block * 64 + 64], placing[rows, :])
        patches = part if patches is None else patches + part
        back_down.append(product(back_merged, project_ref[rows, :], (1, 1)))
    back_down = jnp.concatenate(back_down, axis=0).astype(BF16).astype(F32)
    grad_project = product(patches.astype(BF16), back_merged, (0, 0)).astype(BF16)
    back_section = norm_back(scaled_down, scale_down, back_down * gain_down).astype(BF16)
    back_hidden[...] = product(back_section, outward).astype(BF16)
    slope_rows(expand, back_hidden, 16)
    grad_outward = product(hidden[...], back_section, (0, 0)).astype(BF16)
    grad_inward = product(back_hidden[...], normed, (0, 0)).astype(BF16)
    for third in range(3):
        for core in range(2):
            rows = slice(third * 256 + core * 128, third * 256 + core * 128 + 128)
            left = third * HIDDEN
            grads_ref[core, :, left : left + NARROW] = grad_inward[rows]
            grads_ref[core, :, left + NARROW : left + WIDE] = grad_outward[rows]
            grads_ref[core, :, left + WIDE : left + HIDDEN] = grad_project[rows]


def local_step(*operands):
    smem = pl.BlockSpec(memory_space=pltpu.SMEM)
    vmem = pl.BlockSpec(memory_space=pltpu.VMEM)
    return pl.pallas_call(
        step_kernel,
        in_specs=[smem, smem] + [vmem] * 12,
        out_specs=[vmem, vmem],
        out_shape=[
            jax.ShapeDtypeStruct((TILES, 4, 4, WIDE), BF16),
            jax.ShapeDtypeStruct((2, 128, 3 * HIDDEN), BF16),
        ],
        scratch_shapes=[
            pltpu.VMEM((7, 7, NARROW), F32),
            pltpu.VMEM((7, 7, WIDE), F32),
            pltpu.VMEM((ROWS, NARROW), BF16),
            pltpu.VMEM((ROWS, NARROW), BF16),
            pltpu.VMEM((ROWS, HIDDEN), F32),
            pltpu.VMEM((ROWS, HIDDEN), BF16),
            pltpu.VMEM((ROWS, HIDDEN), BF16),
            pltpu.VMEM((ROWS_TWO, HIDDEN_TWO), F32),
            pltpu.VMEM((ROWS_TWO, HIDDEN_TWO), BF16),
            pltpu.VMEM((ROWS_TWO, HIDDEN_TWO), BF16),
            pltpu.VMEM((ROWS_TWO + 8, WIDE), F32),
            pltpu.VMEM((ROWS_TWO, WIDE), F32),
        ],
        name="local_step",
    )(*operands)


def spread_kernel(parts_ref, out_ref):
    def step(index, carry):
        rows = pl.ds(pl.multiple_of(index * 16, 16), 16)
        total = parts_ref[0, rows, :].astype(F32)
        for part in range(1, parts_ref.shape[0]):
            total = total + parts_ref[part, rows, :].astype(F32)
        for slide in range(8):
            out_ref[index * 8 + slide] = total[2 * slide : 2 * slide + 2].astype(BF16)
        return carry

    lax.fori_loop(0, parts_ref.shape[1] // 16, step, 0)


def spread_sum(parts):
    vmem = pl.BlockSpec(memory_space=pltpu.VMEM)
    return pl.pallas_call(
        spread_kernel,
        in_specs=[vmem],
        out_specs=vmem,
        out_shape=jax.ShapeDtypeStruct((parts.shape[1] // 2, 2, parts.shape[2]), BF16),
        name="spread_sum",
    )(parts)


def exchange(pieces, axis):
    return lax.all_to_all(pieces, axis, split_axis=0, concat_axis=0, tiled=True)


def per_device(
    tile_feats,
    cotangent,
    keep_list,
    tile_plan,
    kernel_one,
    gain_one,
    inward_one,
    outward_one,
    gain_down,
    project_down,
    kernel_two,
    gain_two,
    inward_two,
    outward_two,
):
    features, grads = local_step(
        keep_list,
        tile_plan,
        tile_feats,
        cotangent,
        kernel_one,
        gain_one,
        inward_one,
        outward_one.T,
        gain_down,
        project_down,
        kernel_two,
        gain_two,
        inward_two,
        outward_two,
    )
    own = exchange(grads, "core").astype(F32).sum(axis=0).astype(BF16)
    own = spread_sum(exchange(own.reshape(4, 32, own.shape[1]), "x"))
    own = exchange(own, "z").astype(F32).sum(axis=0)
    share = exchange(jnp.broadcast_to(own, (4, *own.shape)), "rep").sum(axis=0)
    share = share.reshape(2, 3, HIDDEN).transpose(1, 0, 2).reshape(6, HIDDEN)
    return (features, share[:, :NARROW].T, share[:, NARROW:WIDE], share[:, WIDE:])


def solution(mesh):
    split = Mesh(mesh.devices.reshape(4, 16, 2, mesh.shape["rep"]), SLIDE_REP)
    return jax.shard_map(
        per_device,
        mesh=split,
        in_specs=(
            P(SLIDE_REP, None, None, None),
            P(SLIDE_REP, None, None, None),
            P(SLIDE_REP, None),
            P(SLIDE_REP, None),
            P(),
            P(),
            P(),
            P(),
            P(),
            P(),
            P(),
            P(),
            P(),
            P(),
        ),
        out_specs=(P(SLIDE_REP, None, None, None), P(None, SLIDE), P(SLIDE, None), P(SLIDE, None)),
        check_vma=False,
    )
```

```python
import jax
import jax.numpy as jnp
import numpy as np
from jax import lax
from jax.experimental import pallas as pl
from jax.experimental.pallas import tpu as pltpu
from jax.sharding import Mesh
from jax.sharding import PartitionSpec as P

SLIDE = ("x", "z", "core")
SLIDE_REP = ("x", "z", "core", "rep")
F32 = jnp.float32
BF16 = jnp.bfloat16
TILES = 4
CELLS = 16
NARROW = 192
WIDE = 384
HIDDEN = 768
HIDDEN_TWO = 1536
ROWS = 256
ROWS_TWO = 64
HALF_ROOT = 0.7071067811865476
DENSITY = 0.3989422804014327


def product(left, right, contract=(1, 0)):
    return lax.dot_general(
        left, right, (((contract[0],), (contract[1],)), ((), ())), preferred_element_type=F32
    )


def statistics(values, eps=1e-6):
    offset = values - jnp.mean(values, axis=-1, keepdims=True)
    scale = lax.rsqrt(jnp.mean(offset * offset, axis=-1, keepdims=True) + eps)
    return offset * scale, scale


def norm_back(scaled, scale, gained):
    mean = jnp.mean(gained, axis=-1, keepdims=True)
    along = jnp.mean(gained * scaled, axis=-1, keepdims=True)
    return scale * (gained - mean - scaled * along)


def gelu_parts(values):
    below = 0.5 + 0.5 * lax.erf(values * HALF_ROOT)
    return values * below, below + values * (DENSITY * jnp.exp(-0.5 * values * values))


def gelu_columns(rows, weights_ref, hidden_ref, slope_ref, block):
    for left in range(0, slope_ref.shape[1], block):
        columns = slice(left, left + block)
        hidden, slope = gelu_parts(product(rows, weights_ref[:, columns]))
        hidden_ref[:, columns] = hidden.astype(BF16)
        slope_ref[:, columns] = slope


def one_hot(shape, source, source_dim):
    own = lax.broadcasted_iota(jnp.int32, shape, 1 - source_dim)
    index = lax.broadcasted_iota(jnp.int32, shape, source_dim)
    return jnp.where(own == source(index), 1.0, 0.0).astype(BF16)


def hidden_source(place):
    third, rest = place >> 8, place & 255
    core, pair, low = rest >> 7, (rest >> 1) & 63, rest & 1
    return (pair * 2 + core) * 6 + third * 2 + low


def row_source(place):
    tile, x, y = place & 3, (place >> 2) & 3, (place >> 4) & 3
    column, row = (place >> 6) & 1, place >> 7
    return tile * 64 + (2 * y + row) * 8 + 2 * x + column


def cell_source(place):
    return (place & 3) * 16 + (place >> 2)


def tile_place(place):
    return (place & 15) * 4 + (place >> 4)


def conv_one(tile, kernel_ref):
    cell = lax.broadcasted_iota(jnp.int32, (8, NARROW), 0)
    sums = [None] * 8
    for dx in range(-3, 4):
        inside = jnp.logical_and(cell + dx >= 0, cell + dx < 8)
        taps = [jnp.broadcast_to(kernel_ref[dy, dx + 3 : dx + 4, :], (8, NARROW)) for dy in range(7)]
        for source in range(8):
            line = tile[source]
            if dx != 0:
                line = jnp.where(inside, pltpu.roll(line, (-dx) % 8, 0), 0.0)
            for target in range(max(0, source - 3), min(8, source + 4)):
                term = taps[source - target + 3] * line
                sums[target] = term if sums[target] is None else sums[target] + term
    return jnp.concatenate(sums, axis=0)


def conv_two(source_ref, kernel_ref, out_ref, back):
    low = lax.broadcasted_iota(jnp.int32, (8, 128), 0) < 4
    for part in range(WIDE // 128):
        lanes = slice(part * 128, part * 128 + 128)
        cells = []
        for pair in range(CELLS // 2):
            both = source_ref[8 * pair : 8 * pair + 8, lanes]
            swapped = pltpu.roll(both, 4, 0)
            cells.append(jnp.where(low, both, swapped))
            cells.append(jnp.where(low, swapped, both))
        for y in range(4):
            totals = [None, None]
            for fy in range(4):
                dy = (y - fy if back else fy - y) + 3
                taps = [
                    jnp.broadcast_to(kernel_ref[dy, dx : dx + 1, lanes], (8, 128)) for dx in range(7)
                ]
                if back:
                    weights = {dx: jnp.where(low, taps[dx], taps[dx + 1]) for dx in range(6)}
                else:
                    weights = {dx: jnp.where(low, taps[dx], taps[dx - 1]) for dx in range(1, 7)}
                for half in range(2):
                    for fx in range(4):
                        dx = (2 * half - fx if back else fx - 2 * half) + 3
                        term = weights[dx] * cells[fy * 4 + fx]
                        totals[half] = term if totals[half] is None else totals[half] + term
            for half in range(2):
                place = 16 * y + 8 * half
                out_ref[place : place + 8, lanes] = totals[half]


def step_kernel(
    keep_ref,
    plan_ref,
    feats_ref,
    cot_ref,
    kernel_one_ref,
    gain_one_ref,
    inward_one_ref,
    outward_one_ref,
    gain_down_ref,
    project_ref,
    kernel_two_ref,
    gain_two_ref,
    inward_two_ref,
    outward_two_ref,
    placing_ref,
    features_ref,
    grads_ref,
    taps_one,
    taps_two,
    field,
    normed_rows,
    expand,
    hidden,
    back_hidden,
    expand_two,
    hidden_two,
    back_two,
    padded,
    spread,
    cot_cells,
    hidden_back,
    patches_back,
    inward,
    outward,
    placing,
    inward_one,
    outward_one,
    project,
    inward_two,
    outward_two,
    arrived,
):
    copies = []
    pairs = (
        (placing_ref, placing),
        (inward_one_ref, inward_one),
        (outward_one_ref, outward_one),
        (project_ref, project),
        (inward_two_ref, inward_two),
        (outward_two_ref, outward_two),
    )
    for index, (source, target) in enumerate(pairs):
        copies.append(pltpu.make_async_copy(source, target, arrived.at[index]))
        copies[-1].start()
    count = plan_ref[0, 0]
    kept = []
    for tile in range(TILES):
        place = jnp.int32(0)
        for position in range(TILES):
            place = place + jnp.where(keep_ref[0, position] == tile, position, 0)
        kept.append(place < count)
    taps_one[...] = kernel_one_ref[...].astype(F32)
    taps_two[...] = kernel_two_ref[...].astype(F32)
    gain_one = gain_one_ref[...].astype(F32).reshape(1, NARROW)
    gain_down = gain_down_ref[...].astype(F32).reshape(1, NARROW)
    gain_two = gain_two_ref[...].astype(F32).reshape(1, WIDE)

    for tile in range(TILES):
        if tile == 2:
            for copy in copies[:3]:
                copy.wait()
            inward[...] = product(inward_one[...], placing[...]).astype(BF16)
            outward[...] = product(outward_one[...], placing[...]).astype(BF16)
        own = jnp.where(kept[tile], feats_ref[tile].astype(F32), 0.0)
        rows = slice(tile * 64, tile * 64 + 64)
        field[rows, :] = own.reshape(64, NARROW).astype(BF16)
        scaled, _ = statistics(conv_one(own, taps_one))
        normed_rows[rows, :] = (scaled * gain_one).astype(BF16)

    for copy in copies[3:]:
        copy.wait()
    gather_rows = one_hot((ROWS, ROWS), row_source, 0)
    for index in range(CELLS):
        tile, y = index // 4, index % 4
        own = jnp.where(kept[tile], cot_ref[tile, y].astype(F32), 0.0)
        cot_cells[4 * index : 4 * index + 4, :] = own
    gather_cells = one_hot((ROWS_TWO, ROWS_TWO), cell_source, 0)
    flat_cot = product(gather_cells, cot_cells[...].astype(BF16))
    back_two[...] = product(flat_cot.astype(BF16), outward_two[...], (1, 1)).astype(BF16)
    normed = product(gather_rows, normed_rows[...]).astype(BF16)
    field_rows = product(gather_rows, field[...])
    gelu_columns(normed, inward, hidden, expand, 256)
    hidden_back[...] = hidden[...].T
    section = (field_rows + product(hidden[...], outward[...], (1, 1))).astype(BF16).astype(F32)
    scaled_down, scale_down = statistics(section)
    down = (scaled_down * gain_down).astype(BF16)
    merged = patches = None
    for block in range(4):
        rows = slice(block * NARROW, (block + 1) * NARROW)
        own = down[block * 64 : block * 64 + 64]
        part, place = product(own, project[rows, :]), product(own, placing[rows, :])
        merged = part if merged is None else merged + part
        patches = place if patches is None else patches + place
    patches_back[...] = patches.T.astype(BF16)
    merged = merged.astype(BF16).astype(F32)

    padded[...] = merged
    conv_two(padded, taps_two, spread, False)
    scaled_two, scale_two = statistics(spread[...])
    normed_two = (scaled_two * gain_two).astype(BF16)
    gelu_columns(normed_two, inward_two, hidden_two, expand_two, 512)
    features = (merged + product(hidden_two[...], outward_two[...])).astype(BF16)
    scatter_cells = one_hot((ROWS_TWO, ROWS_TWO), tile_place, 0)
    spread[...] = product(scatter_cells, features)
    for index in range(CELLS):
        tile, y = index // 4, index % 4
        own = spread[4 * index : 4 * index + 4, :]
        features_ref[tile, y] = jnp.where(kept[tile], own, 0.0).astype(BF16)

    back_two[...] = (expand_two[...] * back_two[...].astype(F32)).astype(BF16)
    back_normed_two = product(back_two[...], inward_two[...], (1, 1)).astype(BF16).astype(F32)
    padded[...] = norm_back(scaled_two, scale_two, back_normed_two * gain_two)
    conv_two(padded, taps_two, spread, True)
    back_merged = (flat_cot + spread[...]).astype(BF16)

    back_down = []
    for block in range(4):
        rows = slice(block * NARROW, (block + 1) * NARROW)
        back_down.append(product(back_merged, project[rows, :], (1, 1)))
    back_down = jnp.concatenate(back_down, axis=0).astype(BF16).astype(F32)
    grad_project = product(patches_back[...], back_merged).astype(BF16)
    back_section = norm_back(scaled_down, scale_down, back_down * gain_down).astype(BF16)
    for left in range(0, HIDDEN, 256):
        columns = slice(left, left + 256)
        back = product(back_section, outward[:, columns]).astype(BF16).astype(F32)
        back_hidden[:, columns] = (expand[:, columns] * back).astype(BF16)
    grad_outward = product(hidden_back[...], back_section).astype(BF16)
    grad_inward = product(back_hidden[...], normed, (0, 0)).astype(BF16)
    for third in range(3):
        for core in range(2):
            rows = slice(third * 256 + core * 128, third * 256 + core * 128 + 128)
            left = third * HIDDEN
            grads_ref[core, :, left : left + NARROW] = grad_inward[rows]
            grads_ref[core, :, left + NARROW : left + WIDE] = grad_outward[rows]
            grads_ref[core, :, left + WIDE : left + HIDDEN] = grad_project[rows]


def local_step(*operands):
    smem = pl.BlockSpec(memory_space=pltpu.SMEM)
    vmem = pl.BlockSpec(memory_space=pltpu.VMEM)
    hbm = pl.BlockSpec(memory_space=pl.ANY)
    source = hidden_source(np.arange(HIDDEN))
    placing = np.arange(HIDDEN)[:, None] == source[None, :]
    return pl.pallas_call(
        step_kernel,
        in_specs=[smem, smem] + [vmem] * 4 + [hbm, hbm, vmem, hbm, vmem, vmem, hbm, hbm, hbm],
        out_specs=[vmem, vmem],
        out_shape=[
            jax.ShapeDtypeStruct((TILES, 4, 4, WIDE), BF16),
            jax.ShapeDtypeStruct((2, 128, 3 * HIDDEN), BF16),
        ],
        scratch_shapes=[
            pltpu.VMEM((7, 7, NARROW), F32),
            pltpu.VMEM((7, 7, WIDE), F32),
            pltpu.VMEM((ROWS, NARROW), BF16),
            pltpu.VMEM((ROWS, NARROW), BF16),
            pltpu.VMEM((ROWS, HIDDEN), F32),
            pltpu.VMEM((ROWS, HIDDEN), BF16),
            pltpu.VMEM((ROWS, HIDDEN), BF16),
            pltpu.VMEM((ROWS_TWO, HIDDEN_TWO), F32),
            pltpu.VMEM((ROWS_TWO, HIDDEN_TWO), BF16),
            pltpu.VMEM((ROWS_TWO, HIDDEN_TWO), BF16),
            pltpu.VMEM((ROWS_TWO, WIDE), F32),
            pltpu.VMEM((ROWS_TWO, WIDE), F32),
            pltpu.VMEM((ROWS_TWO, WIDE), F32),
            pltpu.VMEM((HIDDEN, ROWS), BF16),
            pltpu.VMEM((HIDDEN, ROWS_TWO), BF16),
            pltpu.VMEM((NARROW, HIDDEN), BF16),
            pltpu.VMEM((NARROW, HIDDEN), BF16),
            pltpu.VMEM((HIDDEN, HIDDEN), BF16),
            pltpu.VMEM((NARROW, HIDDEN), BF16),
            pltpu.VMEM((NARROW, HIDDEN), BF16),
            pltpu.VMEM((HIDDEN, WIDE), BF16),
            pltpu.VMEM((WIDE, HIDDEN_TWO), BF16),
            pltpu.VMEM((HIDDEN_TWO, WIDE), BF16),
            pltpu.SemaphoreType.DMA((6,)),
        ],
        name="local_step",
    )(*operands, jnp.asarray(placing, BF16))


def exchange(pieces, axis):
    return lax.all_to_all(pieces, axis, split_axis=0, concat_axis=0, tiled=True)


def summed(pieces, axis):
    return exchange(pieces, axis).astype(F32).sum(axis=0)


def per_device(
    tile_feats,
    cotangent,
    keep_list,
    tile_plan,
    kernel_one,
    gain_one,
    inward_one,
    outward_one,
    gain_down,
    project_down,
    kernel_two,
    gain_two,
    inward_two,
    outward_two,
):
    features, grads = local_step(
        keep_list,
        tile_plan,
        tile_feats,
        cotangent,
        kernel_one,
        gain_one,
        inward_one,
        outward_one.T,
        gain_down,
        project_down,
        kernel_two,
        gain_two,
        inward_two,
        outward_two,
    )
    own = summed(grads, "core").astype(BF16)
    own = summed(own.reshape(4, 32, own.shape[1]), "x").astype(BF16)
    own = summed(own.reshape(16, 2, own.shape[1]), "z")
    share = exchange(jnp.broadcast_to(own, (4, *own.shape)), "rep").sum(axis=0)
    share = share.reshape(2, 3, HIDDEN).transpose(1, 0, 2).reshape(6, HIDDEN)
    return (features, share[:, :NARROW].T, share[:, NARROW:WIDE], share[:, WIDE:])


def solution(mesh):
    split = Mesh(mesh.devices.reshape(4, 16, 2, mesh.shape["rep"]), SLIDE_REP)
    return jax.shard_map(
        per_device,
        mesh=split,
        in_specs=(
            P(SLIDE_REP, None, None, None),
            P(SLIDE_REP, None, None, None),
            P(SLIDE_REP, None),
            P(SLIDE_REP, None),
            P(),
            P(),
            P(),
            P(),
            P(),
            P(),
            P(),
            P(),
            P(),
            P(),
        ),
        out_specs=(P(SLIDE_REP, None, None, None), P(None, SLIDE), P(SLIDE, None), P(SLIDE, None)),
        check_vma=False,
    )
```

```python
import jax
import jax.numpy as jnp
import numpy as np
from jax import lax
from jax.experimental import pallas as pl
from jax.experimental.pallas import tpu as pltpu
from jax.sharding import Mesh
from jax.sharding import PartitionSpec as P

SLIDE = ("x", "z", "core")
SLIDE_REP = ("x", "z", "core", "rep")
F32 = jnp.float32
BF16 = jnp.bfloat16
TILES = 4
CELLS = 16
NARROW = 192
WIDE = 384
HIDDEN = 768
HIDDEN_TWO = 1536
ROWS = 256
ROWS_TWO = 64
HALF_ROOT = 0.7071067811865476
DENSITY = 0.3989422804014327


def product(left, right, contract=(1, 0)):
    return lax.dot_general(
        left, right, (((contract[0],), (contract[1],)), ((), ())), preferred_element_type=F32
    )


def statistics(values, eps=1e-6):
    offset = values - jnp.mean(values, axis=-1, keepdims=True)
    scale = lax.rsqrt(jnp.mean(offset * offset, axis=-1, keepdims=True) + eps)
    return offset * scale, scale


def norm_back(scaled, scale, gained):
    mean = jnp.mean(gained, axis=-1, keepdims=True)
    along = jnp.mean(gained * scaled, axis=-1, keepdims=True)
    return scale * (gained - mean - scaled * along)


def gelu_parts(values):
    below = 0.5 + 0.5 * lax.erf(values * HALF_ROOT)
    return values * below, below + values * (DENSITY * jnp.exp(-0.5 * values * values))


def gelu_columns(rows, weights_ref, hidden_ref, slope_ref, block, fillers):
    width = slope_ref.shape[1]
    ahead = product(rows, weights_ref[:, :block])
    for left in range(0, width, block):
        own = ahead
        if left + block < width:
            ahead = product(rows, weights_ref[:, left + block : left + 2 * block])
        run_next(fillers)
        for top in range(0, slope_ref.shape[0], 32):
            place = slice(top, top + 32), slice(left, left + block)
            hidden, slope = gelu_parts(own[top : top + 32])
            hidden_ref[place] = hidden.astype(BF16)
            slope_ref[place] = slope


def slope_columns(rows, weights_ref, slope_ref, back_ref, block):
    for left in range(0, slope_ref.shape[1], block):
        back = product(rows, weights_ref[:, left : left + block]).astype(BF16)
        for top in range(0, slope_ref.shape[0], 64):
            place = slice(top, top + 64), slice(left, left + block)
            back_ref[place] = (slope_ref[place] * back[top : top + 64].astype(F32)).astype(BF16)


def one_hot(shape, source, source_dim):
    own = lax.broadcasted_iota(jnp.int32, shape, 1 - source_dim)
    index = lax.broadcasted_iota(jnp.int32, shape, source_dim)
    return jnp.where(own == source(index), 1.0, 0.0).astype(BF16)


def hidden_source(place, mine):
    third, rest = place >> 8, place & 255
    core, pair, low = (rest >> 7) ^ mine, (rest >> 1) & 63, rest & 1
    return (pair * 2 + core) * 6 + third * 2 + low


def row_source(place):
    tile, x, y = place & 3, (place >> 2) & 3, (place >> 4) & 3
    column, row = (place >> 6) & 1, place >> 7
    return tile * 64 + (2 * y + row) * 8 + 2 * x + column


def cell_source(place):
    return (place & 3) * 16 + (place >> 2)


def tile_place(place):
    return (place & 15) * 4 + (place >> 4)


def run_next(fillers):
    if fillers:
        fillers.pop(0)()


def conv_one(tile, kernel_ref, fillers):
    cell = lax.broadcasted_iota(jnp.int32, (8, NARROW), 0)
    sums = [None] * 8
    for dx in range(-3, 4):
        inside = jnp.logical_and(cell + dx >= 0, cell + dx < 8)
        taps = [jnp.broadcast_to(kernel_ref[dy, dx + 3 : dx + 4, :], (8, NARROW)) for dy in range(7)]
        for source in range(8):
            line = tile[source]
            if dx != 0:
                line = jnp.where(inside, pltpu.roll(line, (-dx) % 8, 0), 0.0)
            for target in range(max(0, source - 3), min(8, source + 4)):
                term = taps[source - target + 3] * line
                sums[target] = term if sums[target] is None else sums[target] + term
        run_next(fillers)
    return jnp.concatenate(sums, axis=0)


def conv_two(source_ref, kernel_ref, out_ref, back, fillers):
    low = lax.broadcasted_iota(jnp.int32, (8, 128), 0) < 4
    for part in range(WIDE // 128):
        lanes = slice(part * 128, part * 128 + 128)
        cells = []
        for pair in range(CELLS // 2):
            both = source_ref[8 * pair : 8 * pair + 8, lanes]
            swapped = pltpu.roll(both, 4, 0)
            cells.append(jnp.where(low, both, swapped))
            cells.append(jnp.where(low, swapped, both))
        for y in range(4):
            totals = [None, None]
            for fy in range(4):
                dy = (y - fy if back else fy - y) + 3
                taps = [
                    jnp.broadcast_to(kernel_ref[dy, dx : dx + 1, lanes], (8, 128)) for dx in range(7)
                ]
                if back:
                    weights = {dx: jnp.where(low, taps[dx], taps[dx + 1]) for dx in range(6)}
                else:
                    weights = {dx: jnp.where(low, taps[dx], taps[dx - 1]) for dx in range(1, 7)}
                for half in range(2):
                    for fx in range(4):
                        dx = (2 * half - fx if back else fx - 2 * half) + 3
                        term = weights[dx] * cells[fy * 4 + fx]
                        totals[half] = term if totals[half] is None else totals[half] + term
            for half in range(2):
                place = 16 * y + 8 * half
                out_ref[place : place + 8, lanes] = totals[half]
            run_next(fillers)


def step_kernel(
    keep_ref,
    plan_ref,
    feats_ref,
    cot_ref,
    kernel_one_ref,
    gain_one_ref,
    inward_one_ref,
    outward_one_ref,
    gain_down_ref,
    project_ref,
    kernel_two_ref,
    gain_two_ref,
    inward_two_ref,
    outward_two_ref,
    placing_ref,
    features_ref,
    mine_ref,
    theirs_ref,
    taps_one,
    taps_two,
    field,
    normed_rows,
    expand,
    hidden,
    back_hidden,
    expand_two,
    hidden_two,
    back_two,
    padded,
    spread,
    cot_cells,
    hidden_back,
    patches_back,
    inward,
    outward,
    placing,
    inward_one,
    outward_one,
    project,
    inward_two,
    outward_two,
    arrived,
):
    copies = []
    pairs = (
        (placing_ref.at[lax.axis_index("core")], placing),
        (inward_one_ref, inward_one),
        (outward_one_ref, outward_one),
        (project_ref, project),
        (inward_two_ref, inward_two),
        (outward_two_ref, outward_two),
    )
    for index, (source, target) in enumerate(pairs):
        copies.append(pltpu.make_async_copy(source, target, arrived.at[index]))
        copies[-1].start()
    count = plan_ref[0, 0]
    kept = []
    for tile in range(TILES):
        place = jnp.int32(0)
        for position in range(TILES):
            place = place + jnp.where(keep_ref[0, position] == tile, position, 0)
        kept.append(place < count)
    taps_one[...] = kernel_one_ref[...].astype(F32)
    taps_two[...] = kernel_two_ref[...].astype(F32)
    gain_one = gain_one_ref[...].astype(F32).reshape(1, NARROW)
    gain_down = gain_down_ref[...].astype(F32).reshape(1, NARROW)
    gain_two = gain_two_ref[...].astype(F32).reshape(1, WIDE)

    fillers = []

    def place_columns(source, target, left):
        columns = slice(left, left + 256)
        target[:, columns] = product(source[...], placing[:, columns]).astype(BF16)

    for tile in range(TILES):
        if tile == 2:
            for copy in copies[:3]:
                copy.wait()
            for left in range(0, HIDDEN, 256):
                fillers.append(lambda left=left: place_columns(inward_one, inward, left))
            for left in range(0, HIDDEN, 256):
                fillers.append(lambda left=left: place_columns(outward_one, outward, left))
        own = jnp.where(kept[tile], feats_ref[tile].astype(F32), 0.0)
        rows = slice(tile * 64, tile * 64 + 64)
        field[rows, :] = own.reshape(64, NARROW).astype(BF16)
        scaled, _ = statistics(conv_one(own, taps_one, fillers))
        normed_rows[rows, :] = (scaled * gain_one).astype(BF16)

    for index in range(CELLS):
        tile, y = index // 4, index % 4
        own = jnp.where(kept[tile], cot_ref[tile, y].astype(F32), 0.0)
        cot_cells[4 * index : 4 * index + 4, :] = own
    for copy in copies[3:]:
        copy.wait()
    gather_rows = one_hot((ROWS, ROWS), row_source, 0)
    normed = product(gather_rows, normed_rows[...]).astype(BF16)
    gather_cells = one_hot((ROWS_TWO, ROWS_TWO), cell_source, 0)
    flat_cot = product(gather_cells, cot_cells[...].astype(BF16))
    cot_rows = flat_cot.astype(BF16)

    def cot_columns(left):
        columns = slice(left, left + 512)
        back_two[:, columns] = product(cot_rows, outward_two[columns, :], (1, 1)).astype(BF16)

    fillers = [lambda left=left: cot_columns(left) for left in range(0, HIDDEN_TWO, 512)]
    gelu_columns(normed, inward, hidden, expand, 256, fillers)
    field_rows = product(gather_rows, field[...])
    section = (field_rows + product(hidden[...], outward[...], (1, 1))).astype(BF16).astype(F32)
    merged = None
    down, scaled_down, scale_down = [], [], []
    for block in range(4):
        rows = slice(block * NARROW, (block + 1) * NARROW)
        scaled, scale = statistics(section[block * 64 : block * 64 + 64])
        scaled_down.append(scaled)
        scale_down.append(scale)
        down.append((scaled * gain_down).astype(BF16))
        part = product(down[block], project[rows, :])
        merged = part if merged is None else merged + part
    merged = merged.astype(BF16).astype(F32)

    def place_patches(left):
        columns = slice(left, left + 256)
        total = None
        for block in range(4):
            part = product(down[block], placing[block * NARROW : (block + 1) * NARROW, columns])
            total = part if total is None else total + part
        patches_back[columns, :] = total.T.astype(BF16)

    def turn_hidden(left):
        columns = slice(left, left + 256)
        hidden_back[columns, :] = hidden[:, columns].T

    fillers = []
    for left in range(0, HIDDEN, 256):
        fillers.append(lambda left=left: place_patches(left))
        fillers.append(lambda left=left: turn_hidden(left))
    padded[...] = merged
    conv_two(padded, taps_two, spread, False, fillers)
    scaled_two, scale_two = statistics(spread[...])
    normed_two = (scaled_two * gain_two).astype(BF16)
    gelu_columns(normed_two, inward_two, hidden_two, expand_two, 512, [])
    for left in range(0, HIDDEN_TWO, 512):
        columns = slice(left, left + 512)
        back_two[:, columns] = (expand_two[:, columns] * back_two[:, columns].astype(F32)).astype(BF16)
    back_normed_two = product(back_two[...], inward_two[...], (1, 1)).astype(BF16).astype(F32)

    def feature_columns(left):
        columns = slice(left, left + 128)
        own = product(hidden_two[...], outward_two[:, columns])
        cot_cells[:, columns] = merged[:, columns] + own

    fillers = [lambda left=left: feature_columns(left) for left in range(0, WIDE, 128)]
    padded[...] = norm_back(scaled_two, scale_two, back_normed_two * gain_two)
    conv_two(padded, taps_two, spread, True, fillers)
    back_merged = (flat_cot + spread[...]).astype(BF16)

    back_section = []
    for block in range(4):
        rows = slice(block * NARROW, (block + 1) * NARROW)
        back = product(back_merged, project[rows, :], (1, 1)).astype(BF16).astype(F32)
        back = norm_back(scaled_down[block], scale_down[block], back * gain_down)
        back_section.append(back.astype(BF16))
    back_section = jnp.concatenate(back_section, axis=0)
    slope_columns(back_section, outward, expand, back_hidden, 256)
    scatter_cells = one_hot((ROWS_TWO, ROWS_TWO), tile_place, 0)
    spread[...] = product(scatter_cells, cot_cells[...].astype(BF16))
    for third in range(3):
        hiddens = slice(third * 256, third * 256 + 256)
        left = third * HIDDEN
        grad_project = product(patches_back[hiddens, :], back_merged).astype(BF16)
        grad_outward = product(hidden_back[hiddens, :], back_section).astype(BF16)
        grad_inward = product(back_hidden[:, hiddens], normed, (0, 0)).astype(BF16)
        for core, grads_ref in enumerate((mine_ref, theirs_ref)):
            rows = slice(core * 128, core * 128 + 128)
            grads_ref[:, left : left + NARROW] = grad_inward[rows]
            grads_ref[:, left + NARROW : left + WIDE] = grad_outward[rows]
            grads_ref[:, left + WIDE : left + HIDDEN] = grad_project[rows]
    for index in range(CELLS):
        tile, y = index // 4, index % 4
        own = spread[4 * index : 4 * index + 4, :]
        features_ref[tile, y] = jnp.where(kept[tile], own, 0.0).astype(BF16)


def local_step(*operands):
    smem = pl.BlockSpec(memory_space=pltpu.SMEM)
    vmem = pl.BlockSpec(memory_space=pltpu.VMEM)
    hbm = pl.BlockSpec(memory_space=pl.ANY)
    place = np.arange(HIDDEN)
    placing = np.stack([place[:, None] == hidden_source(place, mine)[None, :] for mine in (0, 1)])
    return pl.pallas_call(
        step_kernel,
        in_specs=[smem, smem] + [vmem] * 4 + [hbm, hbm, vmem, hbm, vmem, vmem, hbm, hbm, hbm],
        out_specs=[vmem, vmem, vmem],
        out_shape=[
            jax.ShapeDtypeStruct((TILES, 4, 4, WIDE), BF16),
            jax.ShapeDtypeStruct((128, 3 * HIDDEN), BF16),
            jax.ShapeDtypeStruct((128, 3 * HIDDEN), BF16),
        ],
        scratch_shapes=[
            pltpu.VMEM((7, 7, NARROW), F32),
            pltpu.VMEM((7, 7, WIDE), F32),
            pltpu.VMEM((ROWS, NARROW), BF16),
            pltpu.VMEM((ROWS, NARROW), BF16),
            pltpu.VMEM((ROWS, HIDDEN), F32),
            pltpu.VMEM((ROWS, HIDDEN), BF16),
            pltpu.VMEM((ROWS, HIDDEN), BF16),
            pltpu.VMEM((ROWS_TWO, HIDDEN_TWO), F32),
            pltpu.VMEM((ROWS_TWO, HIDDEN_TWO), BF16),
            pltpu.VMEM((ROWS_TWO, HIDDEN_TWO), BF16),
            pltpu.VMEM((ROWS_TWO, WIDE), F32),
            pltpu.VMEM((ROWS_TWO, WIDE), F32),
            pltpu.VMEM((ROWS_TWO, WIDE), F32),
            pltpu.VMEM((HIDDEN, ROWS), BF16),
            pltpu.VMEM((HIDDEN, ROWS_TWO), BF16),
            pltpu.VMEM((NARROW, HIDDEN), BF16),
            pltpu.VMEM((NARROW, HIDDEN), BF16),
            pltpu.VMEM((HIDDEN, HIDDEN), BF16),
            pltpu.VMEM((NARROW, HIDDEN), BF16),
            pltpu.VMEM((NARROW, HIDDEN), BF16),
            pltpu.VMEM((HIDDEN, WIDE), BF16),
            pltpu.VMEM((WIDE, HIDDEN_TWO), BF16),
            pltpu.VMEM((HIDDEN_TWO, WIDE), BF16),
            pltpu.SemaphoreType.DMA((6,)),
        ],
        name="local_step",
    )(*operands, jnp.asarray(placing, BF16))


def exchange(pieces, axis):
    return lax.all_to_all(pieces, axis, split_axis=0, concat_axis=0, tiled=True)


def summed(pieces, axis):
    return exchange(pieces, axis).astype(F32).sum(axis=0)


def per_device(
    tile_feats,
    cotangent,
    keep_list,
    tile_plan,
    kernel_one,
    gain_one,
    inward_one,
    outward_one,
    gain_down,
    project_down,
    kernel_two,
    gain_two,
    inward_two,
    outward_two,
):
    features, mine, theirs = local_step(
        keep_list,
        tile_plan,
        tile_feats,
        cotangent,
        kernel_one,
        gain_one,
        inward_one,
        outward_one.T,
        gain_down,
        project_down,
        kernel_two,
        gain_two,
        inward_two,
        outward_two,
    )
    arrived = lax.ppermute(theirs, "core", [(0, 1), (1, 0)])
    own = (mine.astype(F32) + arrived.astype(F32)).astype(BF16)
    own = summed(own.reshape(4, 32, own.shape[1]), "x").astype(BF16)
    own = summed(own.reshape(16, 2, own.shape[1]), "z")
    share = exchange(jnp.broadcast_to(own, (4, *own.shape)), "rep").sum(axis=0)
    share = share.reshape(2, 3, HIDDEN).transpose(1, 0, 2).reshape(6, HIDDEN)
    return (features, share[:, :NARROW].T, share[:, NARROW:WIDE], share[:, WIDE:])


def solution(mesh):
    split = Mesh(mesh.devices.reshape(4, 16, 2, mesh.shape["rep"]), SLIDE_REP)
    return jax.shard_map(
        per_device,
        mesh=split,
        in_specs=(
            P(SLIDE_REP, None, None, None),
            P(SLIDE_REP, None, None, None),
            P(SLIDE_REP, None),
            P(SLIDE_REP, None),
            P(),
            P(),
            P(),
            P(),
            P(),
            P(),
            P(),
            P(),
            P(),
            P(),
        ),
        out_specs=(P(SLIDE_REP, None, None, None), P(None, SLIDE), P(SLIDE, None), P(SLIDE, None)),
        check_vma=False,
    )
```

```python
import jax
import jax.numpy as jnp
import numpy as np
from jax import lax
from jax.experimental import pallas as pl
from jax.experimental.pallas import tpu as pltpu
from jax.sharding import Mesh
from jax.sharding import PartitionSpec as P

SLIDE = ("x", "z", "core")
SLIDE_REP = ("x", "z", "core", "rep")
F32 = jnp.float32
BF16 = jnp.bfloat16
TILES = 4
CELLS = 16
NARROW = 192
WIDE = 384
HIDDEN = 768
HIDDEN_TWO = 1536
ROWS = 256
ROWS_TWO = 64
HALF_ROOT = 0.7071067811865476
DENSITY = 0.3989422804014327


def product(left, right, contract=(1, 0)):
    return lax.dot_general(
        left, right, (((contract[0],), (contract[1],)), ((), ())), preferred_element_type=F32
    )


def statistics(values, eps=1e-6):
    offset = values - jnp.mean(values, axis=-1, keepdims=True)
    scale = lax.rsqrt(jnp.mean(offset * offset, axis=-1, keepdims=True) + eps)
    return offset * scale, scale


def norm_back(scaled, scale, gained):
    mean = jnp.mean(gained, axis=-1, keepdims=True)
    along = jnp.mean(gained * scaled, axis=-1, keepdims=True)
    return scale * (gained - mean - scaled * along)


def gelu_parts(values):
    below = 0.5 + 0.5 * lax.erf(values * HALF_ROOT)
    return values * below, below + values * (DENSITY * jnp.exp(-0.5 * values * values))


def gelu_columns(rows, weights_ref, hidden_ref, slope_ref, block, fillers):
    width = slope_ref.shape[1]
    ahead = product(rows, weights_ref[:, :block])
    for left in range(0, width, block):
        own = ahead
        if left + block < width:
            ahead = product(rows, weights_ref[:, left + block : left + 2 * block])
        run_next(fillers)
        for top in range(0, slope_ref.shape[0], 32):
            place = slice(top, top + 32), slice(left, left + block)
            hidden, slope = gelu_parts(own[top : top + 32])
            hidden_ref[place] = hidden.astype(BF16)
            slope_ref[place] = slope


def slope_columns(rows, weights_ref, slope_ref, back_ref, block):
    for left in range(0, slope_ref.shape[1], block):
        back = product(rows, weights_ref[:, left : left + block]).astype(BF16)
        for top in range(0, slope_ref.shape[0], 64):
            place = slice(top, top + 64), slice(left, left + block)
            back_ref[place] = (slope_ref[place] * back[top : top + 64].astype(F32)).astype(BF16)


def one_hot(shape, source, source_dim):
    own = lax.broadcasted_iota(jnp.int32, shape, 1 - source_dim)
    index = lax.broadcasted_iota(jnp.int32, shape, source_dim)
    return jnp.where(own == source(index), 1.0, 0.0).astype(BF16)


def hidden_source(place, mine):
    third, rest = place >> 8, place & 255
    core, pair, low = (rest >> 7) ^ mine, (rest >> 1) & 63, rest & 1
    return (pair * 2 + core) * 6 + third * 2 + low


def row_source(place):
    tile, x, y = place & 3, (place >> 2) & 3, (place >> 4) & 3
    column, row = (place >> 6) & 1, place >> 7
    return tile * 64 + (2 * y + row) * 8 + 2 * x + column


def cell_source(place):
    return (place & 3) * 16 + (place >> 2)


def tile_place(place):
    return (place & 15) * 4 + (place >> 4)


def run_next(fillers):
    if fillers:
        fillers.pop(0)()


def conv_one(tile, kernel_ref, fillers):
    cell = lax.broadcasted_iota(jnp.int32, (8, NARROW), 0)
    sums = [None] * 8
    for dx in range(-3, 4):
        inside = jnp.logical_and(cell + dx >= 0, cell + dx < 8)
        taps = [jnp.broadcast_to(kernel_ref[dy, dx + 3 : dx + 4, :], (8, NARROW)) for dy in range(7)]
        for source in range(8):
            line = tile[source]
            if dx != 0:
                line = jnp.where(inside, pltpu.roll(line, (-dx) % 8, 0), 0.0)
            for target in range(max(0, source - 3), min(8, source + 4)):
                term = taps[source - target + 3] * line
                sums[target] = term if sums[target] is None else sums[target] + term
        run_next(fillers)
    return jnp.concatenate(sums, axis=0)


def conv_two(source_ref, kernel_ref, out_ref, back, fillers):
    low = lax.broadcasted_iota(jnp.int32, (8, 128), 0) < 4
    for part in range(WIDE // 128):
        lanes = slice(part * 128, part * 128 + 128)
        cells = []
        for pair in range(CELLS // 2):
            both = source_ref[8 * pair : 8 * pair + 8, lanes]
            swapped = pltpu.roll(both, 4, 0)
            cells.append(jnp.where(low, both, swapped))
            cells.append(jnp.where(low, swapped, both))
        for y in range(4):
            totals = [None, None]
            for fy in range(4):
                dy = (y - fy if back else fy - y) + 3
                taps = [
                    jnp.broadcast_to(kernel_ref[dy, dx : dx + 1, lanes], (8, 128)) for dx in range(7)
                ]
                if back:
                    weights = {dx: jnp.where(low, taps[dx], taps[dx + 1]) for dx in range(6)}
                else:
                    weights = {dx: jnp.where(low, taps[dx], taps[dx - 1]) for dx in range(1, 7)}
                for half in range(2):
                    for fx in range(4):
                        dx = (2 * half - fx if back else fx - 2 * half) + 3
                        term = weights[dx] * cells[fy * 4 + fx]
                        totals[half] = term if totals[half] is None else totals[half] + term
            for half in range(2):
                place = 16 * y + 8 * half
                out_ref[place : place + 8, lanes] = totals[half]
            run_next(fillers)


def step_kernel(
    keep_ref,
    plan_ref,
    feats_ref,
    cot_ref,
    kernel_one_ref,
    gain_one_ref,
    inward_one_ref,
    outward_one_ref,
    gain_down_ref,
    project_ref,
    kernel_two_ref,
    gain_two_ref,
    inward_two_ref,
    outward_two_ref,
    placing_ref,
    features_ref,
    mine_ref,
    theirs_ref,
    taps_one,
    taps_two,
    field,
    normed_rows,
    expand,
    hidden,
    back_hidden,
    expand_two,
    hidden_two,
    back_two,
    padded,
    spread,
    cot_cells,
    hidden_back,
    patches_back,
    inward,
    outward,
    placing,
    inward_one,
    outward_one,
    project,
    inward_two,
    outward_two,
    arrived,
):
    copies = []
    pairs = (
        (placing_ref.at[lax.axis_index("core")], placing),
        (inward_one_ref, inward_one),
        (outward_one_ref, outward_one),
        (project_ref, project),
        (inward_two_ref, inward_two),
        (outward_two_ref, outward_two),
    )
    for index, (source, target) in enumerate(pairs):
        copies.append(pltpu.make_async_copy(source, target, arrived.at[index]))
        copies[-1].start()
    count = plan_ref[0, 0]
    kept = []
    for tile in range(TILES):
        place = jnp.int32(0)
        for position in range(TILES):
            place = place + jnp.where(keep_ref[0, position] == tile, position, 0)
        kept.append(place < count)
    taps_one[...] = kernel_one_ref[...].astype(F32)
    taps_two[...] = kernel_two_ref[...].astype(F32)
    gain_one = gain_one_ref[...].astype(F32).reshape(1, NARROW)
    gain_down = gain_down_ref[...].astype(F32).reshape(1, NARROW)
    gain_two = gain_two_ref[...].astype(F32).reshape(1, WIDE)

    fillers = []

    def place_columns(source, target, left):
        columns = slice(left, left + 256)
        target[:, columns] = product(source[...], placing[:, columns]).astype(BF16)

    for tile in range(TILES):
        if tile == 2:
            for copy in copies[:3]:
                copy.wait()
            for left in range(0, HIDDEN, 256):
                fillers.append(lambda left=left: place_columns(inward_one, inward, left))
            for left in range(0, HIDDEN, 256):
                fillers.append(lambda left=left: place_columns(outward_one, outward, left))
        own = jnp.where(kept[tile], feats_ref[tile].astype(F32), 0.0)
        rows = slice(tile * 64, tile * 64 + 64)
        field[rows, :] = own.reshape(64, NARROW).astype(BF16)
        scaled, _ = statistics(conv_one(own, taps_one, fillers))
        normed_rows[rows, :] = (scaled * gain_one).astype(BF16)

    for index in range(CELLS):
        tile, y = index // 4, index % 4
        own = jnp.where(kept[tile], cot_ref[tile, y].astype(F32), 0.0)
        cot_cells[4 * index : 4 * index + 4, :] = own
    for copy in copies[3:]:
        copy.wait()
    gather_rows = one_hot((ROWS, ROWS), row_source, 0)
    normed = product(gather_rows, normed_rows[...]).astype(BF16)
    gather_cells = one_hot((ROWS_TWO, ROWS_TWO), cell_source, 0)
    flat_cot = product(gather_cells, cot_cells[...].astype(BF16))
    cot_rows = flat_cot.astype(BF16)

    def cot_columns(left):
        columns = slice(left, left + 512)
        back_two[:, columns] = product(cot_rows, outward_two[columns, :], (1, 1)).astype(BF16)

    fillers = [lambda left=left: cot_columns(left) for left in range(0, HIDDEN_TWO, 512)]
    gelu_columns(normed, inward, hidden, expand, 256, fillers)
    field_rows = product(gather_rows, field[...])
    section = (field_rows + product(hidden[...], outward[...], (1, 1))).astype(BF16).astype(F32)
    merged = None
    down, scaled_down, scale_down = [], [], []
    for block in range(4):
        rows = slice(block * NARROW, (block + 1) * NARROW)
        scaled, scale = statistics(section[block * 64 : block * 64 + 64])
        scaled_down.append(scaled)
        scale_down.append(scale)
        down.append((scaled * gain_down).astype(BF16))
        part = product(down[block], project[rows, :])
        merged = part if merged is None else merged + part
    merged = merged.astype(BF16).astype(F32)

    def place_patches(left):
        columns = slice(left, left + 256)
        total = None
        for block in range(4):
            part = product(down[block], placing[block * NARROW : (block + 1) * NARROW, columns])
            total = part if total is None else total + part
        patches_back[columns, :] = total.T.astype(BF16)

    def turn_hidden(left):
        columns = slice(left, left + 256)
        hidden_back[columns, :] = hidden[:, columns].T

    fillers = []
    for left in range(0, HIDDEN, 256):
        fillers.append(lambda left=left: place_patches(left))
        fillers.append(lambda left=left: turn_hidden(left))
    padded[...] = merged
    conv_two(padded, taps_two, spread, False, fillers)
    scaled_two, scale_two = statistics(spread[...])
    normed_two = (scaled_two * gain_two).astype(BF16)
    gelu_columns(normed_two, inward_two, hidden_two, expand_two, 512, [])
    for left in range(0, HIDDEN_TWO, 512):
        columns = slice(left, left + 512)
        back_two[:, columns] = (expand_two[:, columns] * back_two[:, columns].astype(F32)).astype(BF16)
    back_normed_two = product(back_two[...], inward_two[...], (1, 1)).astype(BF16).astype(F32)

    def feature_columns(left):
        columns = slice(left, left + 128)
        own = product(hidden_two[...], outward_two[:, columns])
        cot_cells[:, columns] = merged[:, columns] + own

    fillers = [lambda left=left: feature_columns(left) for left in range(0, WIDE, 128)]
    padded[...] = norm_back(scaled_two, scale_two, back_normed_two * gain_two)
    conv_two(padded, taps_two, spread, True, fillers)
    back_merged = (flat_cot + spread[...]).astype(BF16)

    back_section = []
    for block in range(4):
        rows = slice(block * NARROW, (block + 1) * NARROW)
        back = product(back_merged, project[rows, :], (1, 1)).astype(BF16).astype(F32)
        back = norm_back(scaled_down[block], scale_down[block], back * gain_down)
        back_section.append(back.astype(BF16))
    back_section = jnp.concatenate(back_section, axis=0)
    slope_columns(back_section, outward, expand, back_hidden, 256)
    scatter_cells = one_hot((ROWS_TWO, ROWS_TWO), tile_place, 0)
    spread[...] = product(scatter_cells, cot_cells[...].astype(BF16))
    for third in range(3):
        hiddens = slice(third * 256, third * 256 + 256)
        left = third * HIDDEN
        grad_project = product(patches_back[hiddens, :], back_merged).astype(BF16)
        grad_outward = product(hidden_back[hiddens, :], back_section).astype(BF16)
        grad_inward = product(back_hidden[:, hiddens], normed, (0, 0)).astype(BF16)
        for core, grads_ref in enumerate((mine_ref, theirs_ref)):
            rows = slice(core * 128, core * 128 + 128)
            grads_ref[:, left : left + NARROW] = grad_inward[rows]
            grads_ref[:, left + NARROW : left + WIDE] = grad_outward[rows]
            grads_ref[:, left + WIDE : left + HIDDEN] = grad_project[rows]
    for index in range(CELLS):
        tile, y = index // 4, index % 4
        own = spread[4 * index : 4 * index + 4, :]
        features_ref[tile, y] = jnp.where(kept[tile], own, 0.0).astype(BF16)


def local_step(*operands):
    smem = pl.BlockSpec(memory_space=pltpu.SMEM)
    vmem = pl.BlockSpec(memory_space=pltpu.VMEM)
    hbm = pl.BlockSpec(memory_space=pl.ANY)
    place = np.arange(HIDDEN)
    placing = np.stack([place[:, None] == hidden_source(place, mine)[None, :] for mine in (0, 1)])
    return pl.pallas_call(
        step_kernel,
        in_specs=[smem, smem] + [vmem] * 4 + [hbm, hbm, vmem, hbm, vmem, vmem, hbm, hbm, hbm],
        out_specs=[vmem, vmem, vmem],
        out_shape=[
            jax.ShapeDtypeStruct((TILES, 4, 4, WIDE), BF16),
            pltpu.VMEM((128, 3 * HIDDEN), BF16),
            pltpu.VMEM((128, 3 * HIDDEN), BF16),
        ],
        scratch_shapes=[
            pltpu.VMEM((7, 7, NARROW), F32),
            pltpu.VMEM((7, 7, WIDE), F32),
            pltpu.VMEM((ROWS, NARROW), BF16),
            pltpu.VMEM((ROWS, NARROW), BF16),
            pltpu.VMEM((ROWS, HIDDEN), F32),
            pltpu.VMEM((ROWS, HIDDEN), BF16),
            pltpu.VMEM((ROWS, HIDDEN), BF16),
            pltpu.VMEM((ROWS_TWO, HIDDEN_TWO), F32),
            pltpu.VMEM((ROWS_TWO, HIDDEN_TWO), BF16),
            pltpu.VMEM((ROWS_TWO, HIDDEN_TWO), BF16),
            pltpu.VMEM((ROWS_TWO, WIDE), F32),
            pltpu.VMEM((ROWS_TWO, WIDE), F32),
            pltpu.VMEM((ROWS_TWO, WIDE), F32),
            pltpu.VMEM((HIDDEN, ROWS), BF16),
            pltpu.VMEM((HIDDEN, ROWS_TWO), BF16),
            pltpu.VMEM((NARROW, HIDDEN), BF16),
            pltpu.VMEM((NARROW, HIDDEN), BF16),
            pltpu.VMEM((HIDDEN, HIDDEN), BF16),
            pltpu.VMEM((NARROW, HIDDEN), BF16),
            pltpu.VMEM((NARROW, HIDDEN), BF16),
            pltpu.VMEM((HIDDEN, WIDE), BF16),
            pltpu.VMEM((WIDE, HIDDEN_TWO), BF16),
            pltpu.VMEM((HIDDEN_TWO, WIDE), BF16),
            pltpu.SemaphoreType.DMA((6,)),
        ],
        name="local_step",
    )(*operands, jnp.asarray(placing, BF16))


def finish_kernel(parts_ref, inward_ref, outward_ref, project_ref):
    total = parts_ref[0] + parts_ref[1] + parts_ref[2] + parts_ref[3]
    for third in range(3):
        left = third * HIDDEN
        rows = slice(2 * third, 2 * third + 2)
        inward_ref[rows, :] = total[:, left : left + NARROW]
        outward_ref[rows, :] = total[:, left + NARROW : left + WIDE]
        project_ref[rows, :] = total[:, left + WIDE : left + HIDDEN]


def finish(parts):
    vmem = pl.BlockSpec(memory_space=pltpu.VMEM)
    return pl.pallas_call(
        finish_kernel,
        in_specs=[vmem],
        out_specs=[vmem, vmem, vmem],
        out_shape=[jax.ShapeDtypeStruct((6, width), F32) for width in (NARROW, NARROW, WIDE)],
        name="finish",
    )(pltpu.with_memory_space_constraint(parts, pltpu.VMEM))


def exchange(pieces, axis):
    return lax.all_to_all(pieces, axis, split_axis=0, concat_axis=0, tiled=True)


def summed(pieces, axis):
    return exchange(pieces, axis).astype(F32).sum(axis=0)


def per_device(
    tile_feats,
    cotangent,
    keep_list,
    tile_plan,
    kernel_one,
    gain_one,
    inward_one,
    outward_one,
    gain_down,
    project_down,
    kernel_two,
    gain_two,
    inward_two,
    outward_two,
):
    features, mine, theirs = local_step(
        keep_list,
        tile_plan,
        tile_feats,
        cotangent,
        kernel_one,
        gain_one,
        inward_one,
        outward_one.T,
        gain_down,
        project_down,
        kernel_two,
        gain_two,
        inward_two,
        outward_two,
    )
    arrived = lax.ppermute(theirs, "core", [(0, 1), (1, 0)])
    own = (mine.astype(F32) + arrived.astype(F32)).astype(BF16)
    own = summed(own.reshape(4, 32, own.shape[1]), "x").astype(BF16)
    own = summed(own.reshape(16, 2, own.shape[1]), "z")
    inward, outward, project = finish(exchange(jnp.broadcast_to(own, (4, *own.shape)), "rep"))
    return (features, inward.T, outward, project)


def solution(mesh):
    split = Mesh(mesh.devices.reshape(4, 16, 2, mesh.shape["rep"]), SLIDE_REP)
    return jax.shard_map(
        per_device,
        mesh=split,
        in_specs=(
            P(SLIDE_REP, None, None, None),
            P(SLIDE_REP, None, None, None),
            P(SLIDE_REP, None),
            P(SLIDE_REP, None),
            P(),
            P(),
            P(),
            P(),
            P(),
            P(),
            P(),
            P(),
            P(),
            P(),
        ),
        out_specs=(P(SLIDE_REP, None, None, None), P(None, SLIDE), P(SLIDE, None), P(SLIDE, None)),
        check_vma=False,
    )
```

```python
import jax
import jax.numpy as jnp
import numpy as np
from jax import lax
from jax.experimental import pallas as pl
from jax.experimental.pallas import tpu as pltpu
from jax.sharding import Mesh
from jax.sharding import PartitionSpec as P

SLIDE = ("x", "z", "core")
SLIDE_REP = ("x", "z", "core", "rep")
F32 = jnp.float32
BF16 = jnp.bfloat16
TILES = 4
CELLS = 16
NARROW = 192
WIDE = 384
HIDDEN = 768
HIDDEN_TWO = 1536
ROWS = 256
ROWS_TWO = 64
HALF_ROOT = 0.7071067811865476
DENSITY = 0.3989422804014327


def product(left, right, contract=(1, 0)):
    return lax.dot_general(
        left, right, (((contract[0],), (contract[1],)), ((), ())), preferred_element_type=F32
    )


def statistics(values, eps=1e-6):
    offset = values - jnp.mean(values, axis=-1, keepdims=True)
    scale = lax.rsqrt(jnp.mean(offset * offset, axis=-1, keepdims=True) + eps)
    return offset * scale, scale


def norm_back(scaled, scale, gained):
    mean = jnp.mean(gained, axis=-1, keepdims=True)
    along = jnp.mean(gained * scaled, axis=-1, keepdims=True)
    return scale * (gained - mean - scaled * along)


def gelu_parts(values):
    below = 0.5 + 0.5 * lax.erf(values * HALF_ROOT)
    return values * below, below + values * (DENSITY * jnp.exp(-0.5 * values * values))


def gelu_columns(rows, weights_ref, hidden_ref, slope_ref, block, fillers):
    width = slope_ref.shape[1]
    ahead = product(rows, weights_ref[:, :block])
    for left in range(0, width, block):
        own = ahead
        if left + block < width:
            ahead = product(rows, weights_ref[:, left + block : left + 2 * block])
        run_next(fillers)
        for top in range(0, slope_ref.shape[0], 64):
            place = slice(top, top + 64), slice(left, left + block)
            hidden, slope = gelu_parts(own[top : top + 64])
            hidden_ref[place] = hidden.astype(BF16)
            slope_ref[place] = slope


def slope_columns(rows, weights_ref, slope_ref, back_ref, block):
    for left in range(0, slope_ref.shape[1], block):
        back = product(rows, weights_ref[:, left : left + block]).astype(BF16)
        for top in range(0, slope_ref.shape[0], 64):
            place = slice(top, top + 64), slice(left, left + block)
            back_ref[place] = (slope_ref[place] * back[top : top + 64].astype(F32)).astype(BF16)


def one_hot(shape, source, source_dim):
    own = lax.broadcasted_iota(jnp.int32, shape, 1 - source_dim)
    index = lax.broadcasted_iota(jnp.int32, shape, source_dim)
    return jnp.where(own == source(index), 1.0, 0.0).astype(BF16)


def hidden_source(place, mine):
    third, rest = place >> 8, place & 255
    core, pair, low = (rest >> 7) ^ mine, (rest >> 1) & 63, rest & 1
    return (pair * 2 + core) * 6 + third * 2 + low


def row_source(place):
    tile, x, y = place & 3, (place >> 2) & 3, (place >> 4) & 3
    column, row = (place >> 6) & 1, place >> 7
    return tile * 64 + (2 * y + row) * 8 + 2 * x + column


def cell_source(place):
    return (place & 3) * 16 + (place >> 2)


def tile_place(place):
    return (place & 15) * 4 + (place >> 4)


def run_next(fillers):
    if fillers:
        fillers.pop(0)()


def conv_one(tile, kernel_ref, fillers):
    cell = lax.broadcasted_iota(jnp.int32, (8, NARROW), 0)
    sums = [None] * 8
    for dx in range(-3, 4):
        inside = jnp.logical_and(cell + dx >= 0, cell + dx < 8)
        taps = [jnp.broadcast_to(kernel_ref[dy, dx + 3 : dx + 4, :], (8, NARROW)) for dy in range(7)]
        for source in range(8):
            line = tile[source]
            if dx != 0:
                line = jnp.where(inside, pltpu.roll(line, (-dx) % 8, 0), 0.0)
            for target in range(max(0, source - 3), min(8, source + 4)):
                term = taps[source - target + 3] * line
                sums[target] = term if sums[target] is None else sums[target] + term
        run_next(fillers)
    return jnp.concatenate(sums, axis=0)


def conv_two(source_ref, kernel_ref, out_ref, back, fillers):
    low = lax.broadcasted_iota(jnp.int32, (8, 128), 0) < 4
    for part in range(WIDE // 128):
        lanes = slice(part * 128, part * 128 + 128)
        cells = []
        for pair in range(CELLS // 2):
            both = source_ref[8 * pair : 8 * pair + 8, lanes]
            swapped = pltpu.roll(both, 4, 0)
            cells.append(jnp.where(low, both, swapped))
            cells.append(jnp.where(low, swapped, both))
        for y in range(4):
            totals = [None, None]
            for fy in range(4):
                dy = (y - fy if back else fy - y) + 3
                taps = [
                    jnp.broadcast_to(kernel_ref[dy, dx : dx + 1, lanes], (8, 128)) for dx in range(7)
                ]
                if back:
                    weights = {dx: jnp.where(low, taps[dx], taps[dx + 1]) for dx in range(6)}
                else:
                    weights = {dx: jnp.where(low, taps[dx], taps[dx - 1]) for dx in range(1, 7)}
                for half in range(2):
                    for fx in range(4):
                        dx = (2 * half - fx if back else fx - 2 * half) + 3
                        term = weights[dx] * cells[fy * 4 + fx]
                        totals[half] = term if totals[half] is None else totals[half] + term
            for half in range(2):
                place = 16 * y + 8 * half
                out_ref[place : place + 8, lanes] = totals[half]
            run_next(fillers)


def step_kernel(
    keep_ref,
    plan_ref,
    feats_ref,
    cot_ref,
    kernel_one_ref,
    gain_one_ref,
    inward_one_ref,
    outward_one_ref,
    gain_down_ref,
    project_ref,
    kernel_two_ref,
    gain_two_ref,
    inward_two_ref,
    outward_two_ref,
    placing_ref,
    features_ref,
    mine_ref,
    theirs_ref,
    taps_one,
    taps_two,
    field,
    normed_rows,
    expand,
    hidden,
    back_hidden,
    expand_two,
    hidden_two,
    back_two,
    padded,
    spread,
    cot_cells,
    hidden_back,
    patches_back,
    inward,
    outward,
    placing,
    inward_one,
    outward_one,
    project,
    inward_two,
    outward_two,
    arrived,
):
    copies = []
    pairs = (
        (placing_ref.at[lax.axis_index("core")], placing),
        (inward_one_ref, inward_one),
        (outward_one_ref, outward_one),
        (project_ref, project),
        (inward_two_ref, inward_two),
        (outward_two_ref, outward_two),
    )
    for index, (source, target) in enumerate(pairs):
        copies.append(pltpu.make_async_copy(source, target, arrived.at[index]))
        copies[-1].start()
    count = plan_ref[0, 0]
    kept = []
    for tile in range(TILES):
        place = jnp.int32(0)
        for position in range(TILES):
            place = place + jnp.where(keep_ref[0, position] == tile, position, 0)
        kept.append(place < count)
    taps_one[...] = kernel_one_ref[...].astype(F32)
    taps_two[...] = kernel_two_ref[...].astype(F32)
    gain_one = gain_one_ref[...].astype(F32).reshape(1, NARROW)
    gain_down = gain_down_ref[...].astype(F32).reshape(1, NARROW)
    gain_two = gain_two_ref[...].astype(F32).reshape(1, WIDE)

    fillers = []

    def place_columns(source, target, left):
        columns = slice(left, left + 256)
        target[:, columns] = product(source[...], placing[:, columns]).astype(BF16)

    for tile in range(TILES):
        if tile == 2:
            for copy in copies[:3]:
                copy.wait()
            for left in range(0, HIDDEN, 256):
                fillers.append(lambda left=left: place_columns(inward_one, inward, left))
            for left in range(0, HIDDEN, 256):
                fillers.append(lambda left=left: place_columns(outward_one, outward, left))
        own = jnp.where(kept[tile], feats_ref[tile].astype(F32), 0.0)
        rows = slice(tile * 64, tile * 64 + 64)
        field[rows, :] = own.reshape(64, NARROW).astype(BF16)
        scaled, _ = statistics(conv_one(own, taps_one, fillers))
        normed_rows[rows, :] = (scaled * gain_one).astype(BF16)

    for index in range(CELLS):
        tile, y = index // 4, index % 4
        own = jnp.where(kept[tile], cot_ref[tile, y].astype(F32), 0.0)
        cot_cells[4 * index : 4 * index + 4, :] = own
    for copy in copies[3:]:
        copy.wait()
    gather_rows = one_hot((ROWS, ROWS), row_source, 0)
    normed = product(gather_rows, normed_rows[...]).astype(BF16)
    gather_cells = one_hot((ROWS_TWO, ROWS_TWO), cell_source, 0)
    flat_cot = product(gather_cells, cot_cells[...].astype(BF16))
    cot_rows = flat_cot.astype(BF16)

    def cot_columns(left):
        columns = slice(left, left + 512)
        back_two[:, columns] = product(cot_rows, outward_two[columns, :], (1, 1)).astype(BF16)

    fillers = [lambda left=left: cot_columns(left) for left in range(0, HIDDEN_TWO, 512)]
    gelu_columns(normed, inward, hidden, expand, 256, fillers)
    field_rows = product(gather_rows, field[...])
    section = (field_rows + product(hidden[...], outward[...], (1, 1))).astype(BF16).astype(F32)
    merged = None
    down, scaled_down, scale_down = [], [], []
    for block in range(4):
        rows = slice(block * NARROW, (block + 1) * NARROW)
        scaled, scale = statistics(section[block * 64 : block * 64 + 64])
        scaled_down.append(scaled)
        scale_down.append(scale)
        down.append((scaled * gain_down).astype(BF16))
        part = product(down[block], project[rows, :])
        merged = part if merged is None else merged + part
    merged = merged.astype(BF16).astype(F32)

    def place_patches(left):
        columns = slice(left, left + 256)
        total = None
        for block in range(4):
            part = product(down[block], placing[block * NARROW : (block + 1) * NARROW, columns])
            total = part if total is None else total + part
        patches_back[columns, :] = total.T.astype(BF16)

    def turn_hidden(left):
        columns = slice(left, left + 256)
        hidden_back[columns, :] = hidden[:, columns].T

    fillers = []
    for left in range(0, HIDDEN, 256):
        fillers.append(lambda left=left: place_patches(left))
        fillers.append(lambda left=left: turn_hidden(left))
    padded[...] = merged
    conv_two(padded, taps_two, spread, False, fillers)
    scaled_two, scale_two = statistics(spread[...])
    normed_two = (scaled_two * gain_two).astype(BF16)
    gelu_columns(normed_two, inward_two, hidden_two, expand_two, 512, [])
    for left in range(0, HIDDEN_TWO, 512):
        columns = slice(left, left + 512)
        back_two[:, columns] = (expand_two[:, columns] * back_two[:, columns].astype(F32)).astype(BF16)
    back_normed_two = product(back_two[...], inward_two[...], (1, 1)).astype(BF16).astype(F32)

    def feature_columns(left):
        columns = slice(left, left + 128)
        own = product(hidden_two[...], outward_two[:, columns])
        cot_cells[:, columns] = merged[:, columns] + own

    fillers = [lambda left=left: feature_columns(left) for left in range(0, WIDE, 128)]
    padded[...] = norm_back(scaled_two, scale_two, back_normed_two * gain_two)
    conv_two(padded, taps_two, spread, True, fillers)
    back_merged = (flat_cot + spread[...]).astype(BF16)

    back_section = []
    for block in range(4):
        rows = slice(block * NARROW, (block + 1) * NARROW)
        back = product(back_merged, project[rows, :], (1, 1)).astype(BF16).astype(F32)
        back = norm_back(scaled_down[block], scale_down[block], back * gain_down)
        back_section.append(back.astype(BF16))
    back_section = jnp.concatenate(back_section, axis=0)
    slope_columns(back_section, outward, expand, back_hidden, 256)
    scatter_cells = one_hot((ROWS_TWO, ROWS_TWO), tile_place, 0)
    spread[...] = product(scatter_cells, cot_cells[...].astype(BF16))
    for third in range(3):
        hiddens = slice(third * 256, third * 256 + 256)
        left = third * HIDDEN
        grad_project = product(patches_back[hiddens, :], back_merged).astype(BF16)
        grad_outward = product(hidden_back[hiddens, :], back_section).astype(BF16)
        grad_inward = product(back_hidden[:, hiddens], normed, (0, 0)).astype(BF16)
        for core, grads_ref in enumerate((mine_ref, theirs_ref)):
            rows = slice(core * 128, core * 128 + 128)
            grads_ref[:, left : left + NARROW] = grad_inward[rows]
            grads_ref[:, left + NARROW : left + WIDE] = grad_outward[rows]
            grads_ref[:, left + WIDE : left + HIDDEN] = grad_project[rows]
    for index in range(CELLS):
        tile, y = index // 4, index % 4
        own = spread[4 * index : 4 * index + 4, :]
        features_ref[tile, y] = jnp.where(kept[tile], own, 0.0).astype(BF16)


def local_step(*operands):
    smem = pl.BlockSpec(memory_space=pltpu.SMEM)
    vmem = pl.BlockSpec(memory_space=pltpu.VMEM)
    hbm = pl.BlockSpec(memory_space=pl.ANY)
    place = np.arange(HIDDEN)
    placing = np.stack([place[:, None] == hidden_source(place, mine)[None, :] for mine in (0, 1)])
    return pl.pallas_call(
        step_kernel,
        in_specs=[smem, smem] + [vmem] * 4 + [hbm, hbm, vmem, hbm, vmem, vmem, hbm, hbm, hbm],
        out_specs=[vmem, vmem, vmem],
        out_shape=[
            jax.ShapeDtypeStruct((TILES, 4, 4, WIDE), BF16),
            pltpu.VMEM((128, 3 * HIDDEN), BF16),
            pltpu.VMEM((128, 3 * HIDDEN), BF16),
        ],
        scratch_shapes=[
            pltpu.VMEM((7, 7, NARROW), F32),
            pltpu.VMEM((7, 7, WIDE), F32),
            pltpu.VMEM((ROWS, NARROW), BF16),
            pltpu.VMEM((ROWS, NARROW), BF16),
            pltpu.VMEM((ROWS, HIDDEN), F32),
            pltpu.VMEM((ROWS, HIDDEN), BF16),
            pltpu.VMEM((ROWS, HIDDEN), BF16),
            pltpu.VMEM((ROWS_TWO, HIDDEN_TWO), F32),
            pltpu.VMEM((ROWS_TWO, HIDDEN_TWO), BF16),
            pltpu.VMEM((ROWS_TWO, HIDDEN_TWO), BF16),
            pltpu.VMEM((ROWS_TWO, WIDE), F32),
            pltpu.VMEM((ROWS_TWO, WIDE), F32),
            pltpu.VMEM((ROWS_TWO, WIDE), F32),
            pltpu.VMEM((HIDDEN, ROWS), BF16),
            pltpu.VMEM((HIDDEN, ROWS_TWO), BF16),
            pltpu.VMEM((NARROW, HIDDEN), BF16),
            pltpu.VMEM((NARROW, HIDDEN), BF16),
            pltpu.VMEM((HIDDEN, HIDDEN), BF16),
            pltpu.VMEM((NARROW, HIDDEN), BF16),
            pltpu.VMEM((NARROW, HIDDEN), BF16),
            pltpu.VMEM((HIDDEN, WIDE), BF16),
            pltpu.VMEM((WIDE, HIDDEN_TWO), BF16),
            pltpu.VMEM((HIDDEN_TWO, WIDE), BF16),
            pltpu.SemaphoreType.DMA((6,)),
        ],
        name="local_step",
    )(*operands, jnp.asarray(placing, BF16))


def finish_kernel(parts_ref, inward_ref, outward_ref, project_ref):
    total = parts_ref[0].astype(F32)
    for part in range(1, 4):
        total = total + parts_ref[part].astype(F32)
    for third in range(3):
        left = third * HIDDEN
        rows = slice(2 * third, 2 * third + 2)
        inward_ref[rows, :] = total[:, left : left + NARROW]
        outward_ref[rows, :] = total[:, left + NARROW : left + WIDE]
        project_ref[rows, :] = total[:, left + WIDE : left + HIDDEN]


def finish(parts):
    vmem = pl.BlockSpec(memory_space=pltpu.VMEM)
    return pl.pallas_call(
        finish_kernel,
        in_specs=[vmem],
        out_specs=[vmem, vmem, vmem],
        out_shape=[jax.ShapeDtypeStruct((6, width), F32) for width in (NARROW, NARROW, WIDE)],
        name="finish",
    )(pltpu.with_memory_space_constraint(parts, pltpu.VMEM))


def exchange(pieces, axis):
    return lax.all_to_all(pieces, axis, split_axis=0, concat_axis=0, tiled=True)


def summed(pieces, axis):
    return exchange(pieces, axis).astype(F32).sum(axis=0)


def per_device(
    tile_feats,
    cotangent,
    keep_list,
    tile_plan,
    kernel_one,
    gain_one,
    inward_one,
    outward_one,
    gain_down,
    project_down,
    kernel_two,
    gain_two,
    inward_two,
    outward_two,
):
    features, mine, theirs = local_step(
        keep_list,
        tile_plan,
        tile_feats,
        cotangent,
        kernel_one,
        gain_one,
        inward_one,
        outward_one.T,
        gain_down,
        project_down,
        kernel_two,
        gain_two,
        inward_two,
        outward_two,
    )
    arrived = lax.ppermute(theirs, "core", [(0, 1), (1, 0)])
    own = (mine.astype(F32) + arrived.astype(F32)).astype(BF16)
    own = summed(own.reshape(4, 32, own.shape[1]), "x").astype(BF16)
    own = summed(own.reshape(16, 2, own.shape[1]), "z").astype(BF16)
    inward, outward, project = finish(exchange(jnp.broadcast_to(own, (4, *own.shape)), "rep"))
    return (features, inward.T, outward, project)


def solution(mesh):
    split = Mesh(mesh.devices.reshape(4, 16, 2, mesh.shape["rep"]), SLIDE_REP)
    return jax.shard_map(
        per_device,
        mesh=split,
        in_specs=(
            P(SLIDE_REP, None, None, None),
            P(SLIDE_REP, None, None, None),
            P(SLIDE_REP, None),
            P(SLIDE_REP, None),
            P(),
            P(),
            P(),
            P(),
            P(),
            P(),
            P(),
            P(),
            P(),
            P(),
        ),
        out_specs=(P(SLIDE_REP, None, None, None), P(None, SLIDE), P(SLIDE, None), P(SLIDE, None)),
        check_vma=False,
    )
```
